256 devices in a mesh: tm: 128 (over x_hi, z, y, core), mp: 2 (over x_lo).
Axes of the slice: x: 4 (x_hi: 2, x_lo: 2; x = x_hi * 2 + x_lo), y: 4, z: 8, core: 2. Of those that a mesh axis runs over, the one named last changes fastest.
Arguments:
- latent_picture_tokens: bfloat16 [256, 384, 768], P(('tm', 'mp')), may hold values from -6 to 6
- mixing_rescale_factor: float32 [2, 768], replicated, may hold values from 0.1 to 1.9
- joint_lookup_matrix: bfloat16 [2, 768, 1280], P(None, None, 'mp')
- score_scaling: float32 [2, 6], replicated, may hold values from 1 to 24
- mixing_return_matrix: bfloat16 [2, 768, 768], P(None, 'mp'), may hold values from -0.21875 to 0.21875
- perceptron_rescale_factor: float32 [2, 768], replicated, may hold values from 0.1 to 1.9
- widening_matrix: bfloat16 [2, 768, 1536], P(None, None, 'mp'), may hold values from -0.21875 to 0.21875
- narrowing_matrix: bfloat16 [2, 1536, 768], P(None, 'mp'), may hold values from -0.15625 to 0.15625
Outputs:
- result: bfloat16 [256, 384, 768], P(('tm', 'mp'))
The draws below stay inside these ranges and needn't reach their ends.
All inputs are finite; a program needn't handle non-finite values.
Results may differ from the reference program's by a relative error of at most 0.033.
Values may be sent and summed in bfloat16 or wider, within the bound.
No kernel may reach another device: no remote copies, remote signals or barrier semaphores. Data moves between devices by JAX's collectives and lax.ppermute only.
A program may use at most 128 MiB of HBM per device.

```python
import math
import jax
import jax.numpy as jnp
from jax import lax

MODEL_WIDTH = 768
HQ = 6
SHARED_GROUPS = 2
HEAD_SIZE = 128
ASKERS_IN_GROUP = 3
QKV = 1280
FF = 1536
S = 384
LAYER_COUNT = 2
FRAMES = 256


def draw_latent_picture_tokens(key, part):
    second = jax.random.fold_in(key, 1)
    own = jax.random.normal(second, (FRAMES, S, MODEL_WIDTH), jnp.float32)
    content_vectors = own
    return jnp.clip(content_vectors, -6.0, 6.0).astype(jnp.bfloat16)


def draw_joint_lookup_matrix(key, part):
    content_vectors = jax.random.truncated_normal(key, -4.0, 4.0, (LAYER_COUNT, MODEL_WIDTH, QKV), jnp.float32) / math.sqrt(MODEL_WIDTH)
    return content_vectors.astype(jnp.bfloat16)


def draw_score_scaling(key, part):
    spread = jax.random.uniform(key, (LAYER_COUNT, HQ), jnp.float32)
    content_vectors = jnp.exp(spread * math.log(4.0))
    return content_vectors.astype(jnp.float32)


def shard_levels(rng, shape, pieces, smallest, high):
    loudness, own = 1.0, jax.random.fold_in(rng, 6)
    for position, parts in pieces:
        heights = jnp.exp(jax.random.uniform(jax.random.fold_in(own, position), (parts,), jnp.float32, smallest / len(pieces), high / len(pieces)))
        loudness = loudness * jnp.repeat(heights, shape[position] // parts).reshape([-1 if axis == position else 1 for axis in range(len(shape))])
    return loudness


def centred(key, extent, deviation, bound, pieces=(), kind=jnp.bfloat16):
    drawn = deviation * jax.random.normal(key, extent, jnp.float32)
    if pieces:
        drawn = drawn * shard_levels(key, extent, pieces, -0.22, 0.18)
    return jnp.clip(drawn, -bound, bound).astype(kind)


def setup_inputs(seed: int = 0) -> dict:
    arg_keys = jax.random.split(jax.random.key(seed), 9)
    return {
        "latent_picture_tokens": draw_latent_picture_tokens(jax.random.fold_in(arg_keys[8], 71), 0),
        "mixing_rescale_factor": jnp.clip(1.0 + 0.18 * jax.random.normal(arg_keys[1], (LAYER_COUNT, MODEL_WIDTH), jnp.float32), 0.1, 1.9),
        "joint_lookup_matrix": draw_joint_lookup_matrix(jax.random.fold_in(arg_keys[8], 71), 0),
        "score_scaling": draw_score_scaling(jax.random.fold_in(arg_keys[8], 71), 0),
        "mixing_return_matrix": centred(arg_keys[4], (LAYER_COUNT, HQ * HEAD_SIZE, MODEL_WIDTH), (HQ * HEAD_SIZE) ** -0.5, 0.21875, ((1, 2),)),
        "perceptron_rescale_factor": jnp.clip(1.0 + 0.18 * jax.random.normal(arg_keys[5], (LAYER_COUNT, MODEL_WIDTH), jnp.float32), 0.1, 1.9),
        "widening_matrix": centred(arg_keys[6], (LAYER_COUNT, MODEL_WIDTH, FF), MODEL_WIDTH ** -0.5, 0.21875, ((2, 2),)),
        "narrowing_matrix": centred(arg_keys[7], (LAYER_COUNT, FF, MODEL_WIDTH), FF ** -0.5, 0.15625, ((1, 2),)),
    }


def rms_rows(x, gain):
    content_vectors = x.astype(jnp.float32)
    scale = lax.rsqrt(lax.optimization_barrier(jnp.mean(content_vectors * content_vectors, axis=-1, keepdims=True)) + 1e-06)
    return content_vectors * scale * gain.astype(jnp.float32)

def head_norm(t):
    return t * lax.rsqrt(lax.optimization_barrier(jnp.mean(t * t, axis=-1, keepdims=True)) + 1e-06)

def separate_subspaces(flat_vectors, groups, temps):
    count = flat_vectors.shape[0]
    reshaped_rows = flat_vectors.reshape(count, S, groups, ASKERS_IN_GROUP + 2, HEAD_SIZE)
    asker_vectors = head_norm(reshaped_rows[:, :, :, :ASKERS_IN_GROUP, :]) * temps[None, None, :, :, None] / math.sqrt(HEAD_SIZE)
    matcher_vectors = head_norm(reshaped_rows[:, :, :, ASKERS_IN_GROUP, :])
    content_vectors = reshaped_rows[:, :, :, ASKERS_IN_GROUP + 1, :]
    return (asker_vectors.astype(jnp.bfloat16), matcher_vectors.astype(jnp.bfloat16), content_vectors.astype(jnp.bfloat16))

def attend(asker_vectors, matcher_vectors, content_vectors, prior_k, prior_v, anchor_k, anchor_v, frame_ids):
    qf = asker_vectors.astype(jnp.float32)
    own = jnp.einsum('fsgrd,ftgd->fgrst', qf, matcher_vectors.astype(jnp.float32))
    prior = jnp.einsum('fsgrd,ftgd->fgrst', qf, prior_k.astype(jnp.float32))
    anchor = jnp.einsum('fsgrd,tgd->fgrst', qf, anchor_k.astype(jnp.float32))
    lowest = jnp.float32(-1e+30)
    prior = jnp.where((frame_ids >= 1)[:, None, None, None, None], prior, lowest)
    anchor = jnp.where((frame_ids >= 2)[:, None, None, None, None], anchor, lowest)
    top = jnp.maximum(jnp.maximum(lax.optimization_barrier(jnp.max(own, axis=-1, keepdims=True)), lax.optimization_barrier(jnp.max(prior, axis=-1, keepdims=True))), lax.optimization_barrier(jnp.max(anchor, axis=-1, keepdims=True)))
    e_own = jnp.exp(own - top)
    e_prior = jnp.exp(prior - top)
    e_anchor = jnp.exp(anchor - top)
    total = lax.optimization_barrier(jnp.sum(e_own, axis=-1, keepdims=True)) + lax.optimization_barrier(jnp.sum(e_prior, axis=-1, keepdims=True)) + lax.optimization_barrier(jnp.sum(e_anchor, axis=-1, keepdims=True))
    p_own = (e_own / total).astype(jnp.bfloat16).astype(jnp.float32)
    p_prior = (e_prior / total).astype(jnp.bfloat16).astype(jnp.float32)
    p_anchor = (e_anchor / total).astype(jnp.bfloat16).astype(jnp.float32)
    mixed = jnp.einsum('fgrst,ftgd->fsgrd', p_own, content_vectors.astype(jnp.float32))
    mixed = mixed + jnp.einsum('fgrst,ftgd->fsgrd', p_prior, prior_v.astype(jnp.float32))
    mixed = mixed + jnp.einsum('fgrst,tgd->fsgrd', p_anchor, anchor_v.astype(jnp.float32))
    count = asker_vectors.shape[0]
    return mixed.astype(jnp.bfloat16).reshape(count, S, -1)

def reference(latent_picture_tokens, mixing_rescale_factor, joint_lookup_matrix, score_scaling, mixing_return_matrix, perceptron_rescale_factor, widening_matrix, narrowing_matrix):
    state = latent_picture_tokens
    for depth_position in range(LAYER_COUNT):
        normed = rms_rows(state, mixing_rescale_factor[depth_position]).astype(jnp.bfloat16)
        flat_vectors = jnp.einsum('fsd,dc->fsc', normed.astype(jnp.float32), joint_lookup_matrix[depth_position].astype(jnp.float32))
        asker_vectors, matcher_vectors, content_vectors = separate_subspaces(flat_vectors, SHARED_GROUPS, score_scaling[depth_position].reshape(SHARED_GROUPS, ASKERS_IN_GROUP))

        def one_frame(index):
            before = jnp.maximum(index - 1, 0)
            result_frame = attend(asker_vectors[index][None], matcher_vectors[index][None], content_vectors[index][None], matcher_vectors[before][None], content_vectors[before][None], matcher_vectors[0], content_vectors[0], index[None])
            return result_frame[0]
        heads_out = lax.map(one_frame, jnp.arange(FRAMES, dtype=jnp.int32))
        mixed = jnp.einsum('fsc,cd->fsd', heads_out.astype(jnp.float32), mixing_return_matrix[depth_position].astype(jnp.float32))
        state = (state.astype(jnp.float32) + mixed).astype(jnp.bfloat16)
        normed2 = rms_rows(state, perceptron_rescale_factor[depth_position]).astype(jnp.bfloat16)
        hidden = jnp.einsum('fsd,dc->fsc', normed2.astype(jnp.float32), widening_matrix[depth_position].astype(jnp.float32))
        active = jax.nn.gelu(hidden, approximate=True).astype(jnp.bfloat16)
        update = jnp.einsum('fsc,cd->fsd', active.astype(jnp.float32), narrowing_matrix[depth_position].astype(jnp.float32))
        state = (state.astype(jnp.float32) + update).astype(jnp.bfloat16)
    return state
```

```python
import functools
import math

import jax
import jax.numpy as jnp
from jax import lax
from jax.experimental import pallas as pl
from jax.experimental.pallas import tpu as pltpu
from jax.sharding import PartitionSpec as P

HEAD = 128
RATIO = 3
S = 384
D = 768
G = (RATIO + 2) * HEAD
BOTH = ("tm", "mp")
COUNT = 256
BF = jnp.bfloat16
F32 = jnp.float32
QSCALE = 1.0 / (math.sqrt(HEAD) * math.log(2.0))


def place(i):
    return (i >> 7) * 2 + (i & 1), (i >> 2) & 3, (i >> 4) & 7, (i >> 1) & 1


def index(x, y, z, c):
    return ((x >> 1) << 7) | (z << 4) | (y << 2) | (c << 1) | (x & 1)


def pairs(fn):
    return [(i, index(*fn(*place(i)))) for i in range(COUNT)]


ALL4 = (0, 1, 2, 3)
ALL8 = tuple(range(8))


def zodd(z):
    return ((((z + 1) & 7) ^ 1) - 1) & 7


def among(to, xs=ALL4, ys=ALL4, zs=ALL8):
    return [
        (i, j)
        for i, j in pairs(to)
        if place(i)[0] in xs and place(i)[1] in ys and place(i)[2] in zs
    ]


def go_x1(x, y, z, c):
    return x ^ 1, y, z, c


def go_x3(x, y, z, c):
    return x ^ 3, y, z, c


def go_y1(x, y, z, c):
    return x, y ^ 1, z, c


def go_y3(x, y, z, c):
    return x, y ^ 3, z, c


def go_z1(x, y, z, c):
    return x, y, z ^ 1, c


def go_z7(x, y, z, c):
    return x, y, zodd(z), c


X1, X3, Y1, Y3 = pairs(go_x1), pairs(go_x3), pairs(go_y1), pairs(go_y3)
CORE = pairs(lambda x, y, z, c: (x, y, z, 1 - c))
NEXT = [(i, i + 1) for i in range(COUNT - 1)]


def send(v, p):
    return lax.ppermute(v, BOTH, p)


def spread_first(x):
    me = lax.axis_index(BOTH)
    px, py, pz, pc = (me >> 7) * 2 + (me & 1), (me >> 2) & 3, (me >> 4) & 7, (me >> 1) & 1
    half = D // 2
    cur = jnp.where(pc == 0, x[:, :half], send(x[:, half:], CORE))
    got = send(cur[192:], among(go_y3, (0,), (0, 3), (0,)))
    cur = jnp.where(py == 0, cur[:192], got)
    got = send(cur[96:], among(go_y1, (0,), ALL4, (0,)))
    cur = jnp.where((py == 0) | (py == 3), cur[:96], got)
    got = send(cur[48:], among(go_x1, (0, 1), ALL4, (0,)))
    cur = jnp.where(px == 0, cur[:48], got)
    got = send(cur, among(go_x3, ALL4, ALL4, (0,)))
    cur = jnp.where(px < 2, cur, got)
    for i, up, down in ((1, go_z1, go_z7), (2, go_z7, go_z1), (3, go_z1, go_z7)):
        a = send(cur, among(up, ALL4, ALL4, (i - 1, i)))
        b = send(cur, among(down, ALL4, ALL4, ((9 - i) % 8, 8 - i)))
        cur = jnp.where(pz == i, a, jnp.where(pz == 8 - i, b, cur))
    got = send(cur, among(go_z7, ALL4, ALL4, (3, 4)))
    cur = jnp.where(pz == 4, got, cur)
    cur = jnp.concatenate([cur, send(cur, X1)], axis=0)
    cur = jnp.concatenate([cur, send(cur, Y1)], axis=0)
    cur = jnp.concatenate([cur, send(cur, Y3)], axis=0)
    got = send(cur, CORE)
    return jnp.where(
        pc == 0, jnp.concatenate([cur, got], axis=1), jnp.concatenate([got, cur], axis=1)
    )


VMEM = pl.BlockSpec(memory_space=pltpu.VMEM)
SMEM = pl.BlockSpec(memory_space=pltpu.SMEM)
ANY = pl.BlockSpec(memory_space=pl.ANY)
HBM = pl.BlockSpec(memory_space=pltpu.HBM)
NQ, NO, NU = 192, 96, 192
ROWS = NQ + NO + 2 * NU


def params():
    return pltpu.CompilerParams(vmem_limit_bytes=48 << 20)


def cost(flops, nbytes):
    return pl.CostEstimate(flops=flops, bytes_accessed=nbytes, transcendentals=0)


def cut_kernel(l, info, wq, wo, wu, wd, p0, p1, stage, sems):
    core = info[0]
    loads = []
    for j in range(2):
        at = 0
        for i, (src, n) in enumerate(((wq, NQ), (wo, NO), (wu, NU), (wd, NU))):
            rows = pl.ds(pl.multiple_of(core * (2 * n) + j * n, 16), n)
            to = stage.at[j, pl.ds(at, n), pl.ds(0, src.shape[2])]
            c = pltpu.make_async_copy(src.at[l, rows], to, sems.at[4 * j + i])
            c.start()
            loads.append(c)
            at += n
    stores = []
    for j, out in enumerate((p0, p1)):
        for c in loads[4 * j : 4 * j + 4]:
            c.wait()
        c = pltpu.make_async_copy(stage.at[j], out, sems.at[8 + j])
        c.start()
        stores.append(c)
    for c in stores:
        c.wait()


def cut(l, info, weights):
    return pl.pallas_call(
        functools.partial(cut_kernel, l),
        out_shape=[jax.ShapeDtypeStruct((ROWS, D), BF)] * 2,
        in_specs=[SMEM] + [HBM] * 4,
        out_specs=[HBM] * 2,
        scratch_shapes=[pltpu.VMEM((2, ROWS, D), BF), pltpu.SemaphoreType.DMA((10,))],
        compiler_params=params(),
        name="cut",
    )(info, *weights)


def fetch(p):
    a = send(p[0], X1)
    b = send(p[1], X3)
    return a, b, send(a, CORE), send(b, CORE)


def fill(info, quarters, at, n, dst, base, sems, first):
    width = dst.shape[1]
    copies = []
    for j, ref in enumerate(quarters):
        who = info[0] if j < 2 else 1 - info[0]
        row = pl.multiple_of(base + who * (2 * n) + (j % 2) * n, 16)
        c = pltpu.make_async_copy(
            ref.at[pl.ds(at, n), pl.ds(0, width)], dst.at[pl.ds(row, n)], sems.at[first + j]
        )
        c.start()
        copies.append(c)
    return copies


def bring(src, dst, sem):
    c = pltpu.make_async_copy(src, dst, sem)
    c.start()
    return c


def wait(copies):
    for c in copies:
        c.wait()


def rms(t, gain):
    scale = lax.rsqrt(jnp.mean(t * t, axis=-1, keepdims=True) + 1e-06)
    return (t * scale * gain).astype(BF)


def dot(a, b):
    return jnp.dot(a, b, preferred_element_type=F32)


def dot_t(a, b):
    return lax.dot_general(a, b, (((1,), (1,)), ((), ())), preferred_element_type=F32)


def head_norm(t):
    return t * lax.rsqrt(jnp.mean(t * t, axis=-1, keepdims=True) + 1e-06)


def open_qkv(l, info, wq, quarters, w, sems):
    return [bring(wq.at[l], w.at[pl.ds(0, D)], sems.at[4])] + fill(
        info, quarters, 0, NQ, w, D, sems, 0
    )


def scales(info, temps, l, g):
    group = info[2] if g == 0 else 1 - info[2]
    return [temps[l, group * RATIO + r] * QSCALE for r in range(RATIO)]


def project(h, w, ts, q_ref, kv_ref, row, g, keys):
    n = h.shape[0]
    first = 0 if ts is not None else RATIO * HEAD
    last = G if keys else RATIO * HEAD
    raw = dot(h, w[pl.ds(g * D, D), first:last])
    if ts is not None:
        for r in range(RATIO):
            t = head_norm(raw[:, r * HEAD : (r + 1) * HEAD])
            q_ref[pl.ds((g * RATIO + r) * S + row, n), :] = (t * ts[r]).astype(BF)
    if keys:
        at = RATIO * HEAD - first
        kv_ref[pl.ds(row, n), pl.ds(g * 2 * HEAD, HEAD)] = head_norm(
            raw[:, at : at + HEAD]
        ).astype(BF)
        kv_ref[pl.ds(row, n), pl.ds(g * 2 * HEAD + HEAD, HEAD)] = raw[:, at + HEAD :].astype(BF)


QKV_STEP = 192
MIX_STEP = 192
END_STEP = 192


def qkv_kernel(l, info, temps, x_ref, gain, wq, a, b, d, e, q_ref, kv_ref, w, sems):
    copies = open_qkv(l, info, wq, (a, b, d, e), w, sems)
    copies[0].wait()
    hs = []
    for row in range(0, S, QKV_STEP):
        h = rms(x_ref[pl.ds(row, QKV_STEP), :].astype(F32), gain[pl.ds(l, 1), :])
        project(h, w, scales(info, temps, l, 0), q_ref, kv_ref, row, 0, True)
        hs.append(h)
    wait(copies[1:])
    for i, h in enumerate(hs):
        project(h, w, scales(info, temps, l, 1), q_ref, kv_ref, i * QKV_STEP, 1, True)


KV_SHAPE = jax.ShapeDtypeStruct((S, 4 * HEAD), BF)
Q_SHAPE = (2 * RATIO * S, HEAD)
QKV_SCRATCH = [pltpu.VMEM((2 * D, G), BF), pltpu.SemaphoreType.DMA((5,))]


def qkv(l, info, temps, x, gain, wq, quarters):
    return pl.pallas_call(
        functools.partial(qkv_kernel, l),
        out_shape=[jax.ShapeDtypeStruct(Q_SHAPE, BF), KV_SHAPE],
        in_specs=[SMEM, SMEM, VMEM, VMEM] + [HBM] * 5,
        out_specs=[VMEM, VMEM],
        scratch_shapes=QKV_SCRATCH,
        compiler_params=params(),
        cost_estimate=cost(4 * S * D * G, 3 << 20),
        name="qkv",
    )(info, temps, x, gain, wq, *quarters)


def first_kv_kernel(l, info, x_ref, gain, wq, a, b, d, e, kv_ref, w, sems):
    copies = open_qkv(l, info, wq, (a, b, d, e), w, sems)
    hs = []
    for row in range(0, S, QKV_STEP):
        hs.append(rms(x_ref[pl.ds(row, QKV_STEP), :].astype(F32), gain[pl.ds(l, 1), :]))
    wait(copies)
    for g in range(2):
        for i, h in enumerate(hs):
            project(h, w, None, None, kv_ref, i * QKV_STEP, g, True)


def first_kv(l, info, x, gain, wq, quarters):
    return pl.pallas_call(
        functools.partial(first_kv_kernel, l),
        out_shape=KV_SHAPE,
        in_specs=[SMEM, VMEM, VMEM] + [HBM] * 5,
        out_specs=VMEM,
        scratch_shapes=QKV_SCRATCH,
        compiler_params=params(),
        cost_estimate=cost(8 * S * D * HEAD, 3 << 20),
        name="first_kv",
    )(info, x, gain, wq, *quarters)


def mix(q_ref, kvs, columns, shuts, o_ref, ext, g):
    for i, (kv, at) in enumerate(zip(kvs, columns)):
        ext[i, :, :HEAD] = kv[:, at + HEAD : at + 2 * HEAD]
        ext[i, :, HEAD:] = jnp.ones((S, HEAD), BF)
    for r in range(RATIO):
        for row in range(0, S, MIX_STEP):
            q = q_ref[pl.ds((g * RATIO + r) * S + row, MIX_STEP), :]
            scores = [dot_t(q, kv[:, at : at + HEAD]) for kv, at in zip(kvs, columns)]
            tops = [s.max(axis=-1, keepdims=True) for s in scores]
            top = tops[0]
            for t, shut in zip(tops[1:], shuts[1:]):
                top = jnp.maximum(top, t - shut)
            acc = None
            for i, s in enumerate(scores):
                base = top if i == 0 else top + shuts[i]
                part = dot(jnp.exp2(s - base).astype(BF), ext[i])
                acc = part if acc is None else acc + part
            o_ref[pl.ds(row, MIX_STEP), pl.ds((g * RATIO + r) * HEAD, HEAD)] = (
                acc[:, :HEAD] / acc[:, HEAD:]
            ).astype(BF)


def attend_kernel(info, q, kv, prior, first, o_ref, ext):
    shuts = [None, jnp.where(info[1] >= 1, 0.0, 1e30), jnp.where(info[1] >= 2, 0.0, 1e30)]
    for g in range(2):
        mine, theirs = g * 2 * HEAD, (1 - g) * 2 * HEAD
        mix(q, (kv, prior, first), (mine, theirs, mine), shuts, o_ref, ext, g)


def attend(info, q, kv, prior, first):
    return pl.pallas_call(
        attend_kernel,
        out_shape=jax.ShapeDtypeStruct((S, D), BF),
        in_specs=[SMEM] + [VMEM] * 4,
        out_specs=VMEM,
        scratch_shapes=[pltpu.VMEM((3, S, 2 * HEAD), BF)],
        compiler_params=params(),
        cost_estimate=cost(4 * S * 3 * S * D, 4 << 20),
        name="attend",
    )(info, q, kv, prior, first)


def first_mix_kernel(info, temps, x_ref, kv, gain, wq, a, b, d, e, o_ref, w, sems, q, ext):
    copies = open_qkv(0, info, wq, (a, b, d, e), w, sems)
    hs = []
    for row in range(0, S, QKV_STEP):
        hs.append(rms(x_ref[pl.ds(row, QKV_STEP), :].astype(F32), gain[pl.ds(0, 1), :]))
    wait(copies)
    for g in range(2):
        for i, h in enumerate(hs):
            project(h, w, scales(info, temps, 0, g), q, None, i * QKV_STEP, g, False)
        mix(q, (kv,), (g * 2 * HEAD,), [None], o_ref, ext, g)


def first_mix(info, temps, x, kv, gain, wq, quarters):
    return pl.pallas_call(
        first_mix_kernel,
        out_shape=jax.ShapeDtypeStruct((S, D), BF),
        in_specs=[SMEM] * 2 + [VMEM] * 3 + [HBM] * 5,
        out_specs=VMEM,
        scratch_shapes=QKV_SCRATCH
        + [pltpu.VMEM(Q_SHAPE, BF), pltpu.VMEM((1, S, 2 * HEAD), BF)],
        compiler_params=params(),
        cost_estimate=cost(4 * S * S * D + 4 * S * D * 3 * HEAD, 4 << 20),
        name="first_mix",
    )(info, temps, x, kv, gain, wq, *quarters)


def finish_kernel(
    l, info, x_ref, o_ref, gain, wo, wu, wd, a, b, d, e, out, back, up, down, sems
):
    quarters = (a, b, d, e)
    copies = [bring(wo.at[l], back.at[pl.ds(0, S)], sems.at[12])]
    copies += fill(info, quarters, NQ, NO, back, S, sems, 0)
    more = [bring(wu.at[l], up.at[pl.ds(0, D)], sems.at[13])]
    more += fill(info, quarters, NQ + NO, NU, up, D, sems, 4)
    more += [bring(wd.at[l], down.at[pl.ds(0, D)], sems.at[14])]
    more += fill(info, quarters, NQ + NO + NU, NU, down, D, sems, 8)
    wait(copies)
    for n, row in enumerate(range(0, S, END_STEP)):
        rows = pl.ds(row, END_STEP)
        x = (x_ref[rows, :].astype(F32) + dot(o_ref[rows, :], back[...])).astype(BF)
        h = rms(x.astype(F32), gain[pl.ds(l, 1), :])
        if n == 0:
            wait(more)
        y = x.astype(F32)
        for g in range(2):
            t = jax.nn.gelu(dot(h, up[pl.ds(g * D, D), :]), approximate=True).astype(BF)
            y = y + dot(t, down[pl.ds(g * D, D), :])
        out[rows, :] = y.astype(BF)


def finish(l, info, x, o, gain, own, quarters):
    return pl.pallas_call(
        functools.partial(finish_kernel, l),
        out_shape=jax.ShapeDtypeStruct((S, D), BF),
        in_specs=[SMEM] + [VMEM] * 3 + [HBM] * 7,
        out_specs=VMEM,
        scratch_shapes=[
            pltpu.VMEM((D, D), BF),
            pltpu.VMEM((2 * D, D), BF),
            pltpu.VMEM((2 * D, D), BF),
            pltpu.SemaphoreType.DMA((15,)),
        ],
        compiler_params=params(),
        cost_estimate=cost(2 * S * D * (D + 4 * D), 9 << 20),
        name="finish",
    )(info, x, o, gain, *own, *quarters)


def shards(x, gain_a, wqkv, temps, wout, gain_m, wup, wdown):
    me = lax.axis_index(BOTH)
    info = jnp.stack([(me >> 1) & 1, me, me & 1]).astype(jnp.int32)
    x = x[0]
    own = (wout, wup, wdown)
    p = cut(0, info, (wqkv, *own))
    xb, p = lax.optimization_barrier((x, p))
    w0 = fetch(p)
    first = spread_first(xb)
    p = cut(1, info, (wqkv, *own))
    p, _ = lax.optimization_barrier((p, w0[1]))
    w1 = fetch(p)

    q, kv = qkv(0, info, temps, x, gain_a, wqkv, w0)
    prior = send(kv, NEXT)
    kv0 = first_kv(0, info, first, gain_a, wqkv, w0)
    o = attend(info, q, kv, prior, kv0)
    x = finish(0, info, x, o, gain_m, own, w0)
    q, kv = qkv(1, info, temps, x, gain_a, wqkv, w1)
    prior = send(kv, NEXT)
    o = first_mix(info, temps, first, kv0, gain_a, wqkv, w0)
    first = finish(0, info, first, o, gain_m, own, w0)
    kv0 = first_kv(1, info, first, gain_a, wqkv, w1)
    o = attend(info, q, kv, prior, kv0)
    return finish(1, info, x, o, gain_m, own, w1)[None]


def solution(mesh):
    in_specs = (
        P(BOTH, None, None),
        P(),
        P(None, None, "mp"),
        P(),
        P(None, "mp", None),
        P(),
        P(None, None, "mp"),
        P(None, "mp", None),
    )
    return jax.shard_map(
        shards, mesh=mesh, in_specs=in_specs, out_specs=P(BOTH, None, None), check_vma=False
    )
```

```python
import functools
import math

import jax
import jax.numpy as jnp
from jax import lax
from jax.experimental import pallas as pl
from jax.experimental.pallas import tpu as pltpu
from jax.sharding import PartitionSpec as P

HEAD = 128
RATIO = 3
S = 384
D = 768
G = (RATIO + 2) * HEAD
BOTH = ("tm", "mp")
COUNT = 256
BF = jnp.bfloat16
F32 = jnp.float32
QSCALE = 1.0 / (math.sqrt(HEAD) * math.log(2.0))


def place(i):
    return (i >> 7) * 2 + (i & 1), (i >> 2) & 3, (i >> 4) & 7, (i >> 1) & 1


def index(x, y, z, c):
    return ((x >> 1) << 7) | (z << 4) | (y << 2) | (c << 1) | (x & 1)


def pairs(fn):
    return [(i, index(*fn(*place(i)))) for i in range(COUNT)]


def zodd(z):
    return ((((z + 1) & 7) ^ 1) - 1) & 7


def go_x1(x, y, z, c):
    return x ^ 1, y, z, c


def go_x3(x, y, z, c):
    return x ^ 3, y, z, c


def go_y1(x, y, z, c):
    return x, y ^ 1, z, c


def go_y3(x, y, z, c):
    return x, y ^ 3, z, c


def go_z1(x, y, z, c):
    return x, y, z ^ 1, c


def go_z7(x, y, z, c):
    return x, y, zodd(z), c


X1, X3 = pairs(go_x1), pairs(go_x3)
EVEN_X1, EVEN_X3, EVEN_Y1, EVEN_Y3, EVEN_Z1, EVEN_Z7 = (
    [(i, j) for i, j in pairs(go) if place(i)[3] == 0]
    for go in (go_x1, go_x3, go_y1, go_y3, go_z1, go_z7)
)
CORE = pairs(lambda x, y, z, c: (x, y, z, 1 - c))
NEXT = [(i, i + 1) for i in range(COUNT - 1)]


def send(v, p):
    return lax.ppermute(v, BOTH, p)


def spread_first(x):
    me = lax.axis_index(BOTH)
    px, py, pz, pc = (me >> 7) * 2 + (me & 1), (me >> 2) & 3, (me >> 4) & 7, (me >> 1) & 1
    cur = jnp.where(py == 0, x[:192], send(x[192:], EVEN_Y3))
    cur = jnp.where((py == 0) | (py == 3), cur[:96], send(cur[96:], EVEN_Y1))
    cur = jnp.where(px == 0, cur, send(cur, EVEN_X1))
    cur = jnp.where(px < 2, cur, send(cur, EVEN_X3))
    mark = cur
    for i, up, down in ((1, EVEN_Z1, EVEN_Z7), (2, EVEN_Z7, EVEN_Z1), (3, EVEN_Z1, EVEN_Z7)):
        a, b = send(cur, up), send(cur, down)
        cur = jnp.where(pz == i, a, jnp.where(pz == 8 - i, b, cur))
    cur = jnp.where(pz == 4, send(cur, EVEN_Z7), cur)
    cur = jnp.concatenate([cur, send(cur, EVEN_Y1)], axis=0)
    cur = jnp.concatenate([cur, send(cur, EVEN_Y3)], axis=0)
    return jnp.where(pc == 0, cur, send(cur, CORE)), mark


VMEM = pl.BlockSpec(memory_space=pltpu.VMEM)
SMEM = pl.BlockSpec(memory_space=pltpu.SMEM)
ANY = pl.BlockSpec(memory_space=pl.ANY)
HBM = pl.BlockSpec(memory_space=pltpu.HBM)
NQ, NO, NU = 192, 96, 192
ROWS = NO + 2 * NU


def params(mib=40):
    return pltpu.CompilerParams(vmem_limit_bytes=mib << 20)


def cost(flops, nbytes):
    return pl.CostEstimate(flops=flops, bytes_accessed=nbytes, transcendentals=0)


def cut_kernel(info, wq, wo, wu, wd, *refs):
    outs, stage_q, stage_r, sems = refs[:8], refs[8], refs[9], refs[10]
    core = info[0]
    loads = []
    for l in range(2):
        for j in range(2):
            at = 0
            for i, (src, n) in enumerate(((wq, NQ), (wo, NO), (wu, NU), (wd, NU))):
                rows = pl.ds(pl.multiple_of(core * (2 * n) + j * n, 16), n)
                if i == 0:
                    to = stage_q.at[2 * l + j]
                else:
                    to = stage_r.at[2 * l + j, pl.ds(at, n)]
                    at += n
                loads.append(bring(src.at[l, rows], to, sems.at[8 * l + 4 * j + i]))
    stores = []
    for l in range(2):
        for j in range(2):
            k = 2 * l + j
            loads[4 * k].wait()
            stores.append(bring(stage_q.at[k], outs[4 * l + j], sems.at[16 + 2 * k]))
            wait(loads[4 * k + 1 : 4 * k + 4])
            stores.append(bring(stage_r.at[k], outs[4 * l + 2 + j], sems.at[17 + 2 * k]))
    wait(stores)


def cut(info, weights):
    shapes = ([jax.ShapeDtypeStruct((NQ, G), BF)] * 2 + [jax.ShapeDtypeStruct((ROWS, D), BF)] * 2) * 2
    return pl.pallas_call(
        cut_kernel,
        out_shape=shapes,
        in_specs=[SMEM] + [HBM] * 4,
        out_specs=[HBM] * 8,
        scratch_shapes=[
            pltpu.VMEM((4, NQ, G), BF),
            pltpu.VMEM((4, ROWS, D), BF),
            pltpu.SemaphoreType.DMA((24,)),
        ],
        compiler_params=params(63),
        cost_estimate=cost(0, 16 << 20),
        name="cut",
    )(info, *weights)


def fetch(p, after=None):
    if after is not None:
        p, _ = lax.optimization_barrier((p, after))
    return send(p[0], X1), send(p[1], X3)


def swap(ab, after=None):
    if after is not None:
        ab, _ = lax.optimization_barrier((ab, after))
    return *ab, send(ab[0], CORE), send(ab[1], CORE)


def fill(info, quarters, at, n, dst, base, sems, first):
    width = dst.shape[1]
    copies = []
    for j, ref in enumerate(quarters):
        who = info[0] if j < 2 else 1 - info[0]
        row = pl.multiple_of(base + who * (2 * n) + (j % 2) * n, 16)
        c = pltpu.make_async_copy(
            ref.at[pl.ds(at, n), pl.ds(0, width)], dst.at[pl.ds(row, n)], sems.at[first + j]
        )
        c.start()
        copies.append(c)
    return copies


def bring(src, dst, sem):
    c = pltpu.make_async_copy(src, dst, sem)
    c.start()
    return c


def wait(copies):
    for c in copies:
        c.wait()


def rms(t, gain):
    scale = lax.rsqrt(jnp.mean(t * t, axis=-1, keepdims=True) + 1e-06)
    return (t * scale * gain).astype(BF)


def dot(a, b):
    return jnp.dot(a, b, preferred_element_type=F32)


def dot_t(a, b):
    return lax.dot_general(a, b, (((1,), (1,)), ((), ())), preferred_element_type=F32)


def head_norm(t):
    return t * lax.rsqrt(jnp.mean(t * t, axis=-1, keepdims=True) + 1e-06)


def open_qkv(l, info, wq, quarters, w, sems):
    return [bring(wq.at[l], w.at[pl.ds(0, D)], sems.at[4])] + fill(
        info, quarters, 0, NQ, w, D, sems, 0
    )


def open_rest(l, info, own, quarters, back, up, down, sems):
    wo, wu, wd = own
    copies = [bring(wo.at[l], back.at[pl.ds(0, S)], sems.at[12])]
    copies += fill(info, quarters, 0, NO, back, S, sems, 0)
    copies += [bring(wu.at[l], up.at[pl.ds(0, D)], sems.at[13])]
    copies += fill(info, quarters, NO, NU, up, D, sems, 4)
    copies += [bring(wd.at[l], down.at[pl.ds(0, D)], sems.at[14])]
    copies += fill(info, quarters, NO + NU, NU, down, D, sems, 8)
    return copies


def scales(info, temps, l, g):
    group = info[2] if g == 0 else 1 - info[2]
    return [temps[l, group * RATIO + r] * QSCALE for r in range(RATIO)]


def project(h, w, ts, q_ref, kv_ref, row, g, keys):
    n = h.shape[0]
    first = 0 if ts is not None else RATIO * HEAD
    last = G if keys else RATIO * HEAD
    raw = dot(h, w[pl.ds(g * D, D), first:last])
    if ts is not None:
        for r in range(RATIO):
            t = head_norm(raw[:, r * HEAD : (r + 1) * HEAD])
            q_ref[pl.ds((g * RATIO + r) * S + row, n), :] = (t * ts[r]).astype(BF)
    if keys:
        at = RATIO * HEAD - first
        kv_ref[pl.ds(row, n), pl.ds(g * 2 * HEAD, HEAD)] = head_norm(
            raw[:, at : at + HEAD]
        ).astype(BF)
        kv_ref[pl.ds(row, n), pl.ds(g * 2 * HEAD + HEAD, HEAD)] = raw[:, at + HEAD :].astype(BF)


QKV_STEP = 192
MIX_STEP = 192
END_STEP = 192
WQ = jax.ShapeDtypeStruct((2 * D, G), BF)
REST = [jax.ShapeDtypeStruct((n * D, D), BF) for n in (1, 2, 2)]
KV = jax.ShapeDtypeStruct((S, 4 * HEAD), BF)
Q = jax.ShapeDtypeStruct((2 * RATIO * S, HEAD), BF)
X = jax.ShapeDtypeStruct((S, D), BF)


def normed(l, x_ref, gain):
    return [
        rms(x_ref[pl.ds(row, QKV_STEP), :].astype(F32), gain[pl.ds(l, 1), :])
        for row in range(0, S, QKV_STEP)
    ]


def all_project(l, info, temps, hs, w, q_ref, kv_ref, g):
    ts = None if q_ref is None else scales(info, temps, l, g)
    for i, h in enumerate(hs):
        project(h, w, ts, q_ref, kv_ref, i * QKV_STEP, g, kv_ref is not None)


def call(body, name, outs, ins, flops, scratch=()):
    return pl.pallas_call(
        body,
        out_shape=outs,
        in_specs=[spec for spec, _ in ins],
        out_specs=[VMEM] * len(outs),
        scratch_shapes=list(scratch),
        compiler_params=params(16),
        cost_estimate=cost(flops, 8 << 20),
        name=name,
    )(*[v for _, v in ins])


def qkv_kernel(info, temps, x_ref, gain, wq, a, b, d, e, q_ref, kv_ref, w, sems):
    copies = open_qkv(0, info, wq, (a, b, d, e), w, sems)
    copies[0].wait()
    hs = normed(0, x_ref, gain)
    all_project(0, info, temps, hs, w, q_ref, kv_ref, 0)
    wait(copies[1:])
    all_project(0, info, temps, hs, w, q_ref, kv_ref, 1)


def prepare_kernel(l, info, *refs):
    wait(open_rest(l, info, refs[:3], refs[3:7], *refs[7:10], refs[10]))


def spread_values(kv, at, ext, i):
    ext[i, :, :HEAD] = kv[:, at + HEAD : at + 2 * HEAD]
    ext[i, :, HEAD:] = jnp.ones((S, HEAD), BF)


def blocks():
    return [(r, row) for r in range(RATIO) for row in range(0, S, MIX_STEP)]


def soften(q, kvs, columns, shuts, ext, old=None):
    scores = [dot_t(q, kv[:, at : at + HEAD]) for kv, at in zip(kvs, columns)]
    top = None if old is None else old[1]
    for s, shut in zip(scores, shuts):
        t = s.max(axis=-1, keepdims=True)
        t = t if shut is None else t - shut
        top = t if top is None else jnp.maximum(top, t)
    acc = None if old is None else old[0] * jnp.exp2(old[1] - top)
    for i, (s, shut) in enumerate(zip(scores, shuts)):
        base = top if shut is None else top + shut
        part = dot(jnp.exp2(s - base).astype(BF), ext[i])
        acc = part if acc is None else acc + part
    return acc, top


def close(acc):
    return (acc[:, :HEAD] / acc[:, HEAD:]).astype(BF)


def mix(q_ref, kvs, columns, shuts, o_ref, ext, g):
    for i, (kv, at) in enumerate(zip(kvs, columns)):
        spread_values(kv, at, ext, i)
    for r, row in blocks():
        h = g * RATIO + r
        acc, _ = soften(q_ref[pl.ds(h * S + row, MIX_STEP), :], kvs, columns, shuts, ext)
        o_ref[pl.ds(row, MIX_STEP), pl.ds(h * HEAD, HEAD)] = close(acc)


def shut_if(bad):
    return jnp.where(bad, 1e30, 0.0)


def begin_kernel(info, q_ref, kv, prior, acc_ref, top_ref, ext):
    shuts = [None, shut_if(info[1] < 1)]
    for g in range(2):
        columns = (g * 2 * HEAD, (1 - g) * 2 * HEAD)
        for i, (v, at) in enumerate(zip((kv, prior), columns)):
            spread_values(v, at, ext, i)
        for r, row in blocks():
            rows = pl.ds((g * RATIO + r) * S + row, MIX_STEP)
            acc, top = soften(q_ref[rows, :], (kv, prior), columns, shuts, ext)
            acc_ref[rows, :] = acc
            top_ref[rows, :] = jnp.broadcast_to(top, (MIX_STEP, HEAD))


def finish_rows(l, x_ref, o_ref, gain, back, up, down, out):
    for row in range(0, S, END_STEP):
        rows = pl.ds(row, END_STEP)
        x = (x_ref[rows, :].astype(F32) + dot(o_ref[rows, :], back[...])).astype(BF)
        h = rms(x.astype(F32), gain[pl.ds(l, 1), :])
        y = x.astype(F32)
        for g in range(2):
            t = jax.nn.gelu(dot(h, up[pl.ds(g * D, D), :]), approximate=True).astype(BF)
            y = y + dot(t, down[pl.ds(g * D, D), :])
        out[rows, :] = y.astype(BF)


def own_kernel(
    info, temps, first, x_ref, q_ref, acc_ref, top_ref, gain_a, gain_m, wq0, back, up, down,
    wq, a, b, d, e, out, q_out, kv_out, kv0, w1, o, ext, sems,
):
    copies = open_qkv(1, info, wq, (a, b, d, e), w1, sems)
    hs = normed(0, first, gain_a)
    shuts = [shut_if(info[1] < 2)]
    for g in range(2):
        all_project(0, info, temps, hs, wq0, None, kv0, g)
        at = g * 2 * HEAD
        spread_values(kv0, at, ext, 0)
        for r, row in blocks():
            h = g * RATIO + r
            rows = pl.ds(h * S + row, MIX_STEP)
            old = (acc_ref[rows, :], top_ref[rows, :1])
            acc, _ = soften(q_ref[rows, :], (kv0,), (at,), shuts, ext, old)
            o[pl.ds(row, MIX_STEP), pl.ds(h * HEAD, HEAD)] = close(acc)
    finish_rows(0, x_ref, o, gain_m, back, up, down, out)
    hs = normed(1, out, gain_a)
    wait(copies)
    for g in range(2):
        all_project(1, info, temps, hs, w1, q_out, kv_out, g)


def first_kernel(
    info, temps, first, kv0, gain_a, gain_m, wq0, back, up, down, wq1,
    kv_out, q, o, x, ext,
):
    hs = normed(0, first, gain_a)
    for g in range(2):
        all_project(0, info, temps, hs, wq0, q, None, g)
        mix(q, (kv0,), (g * 2 * HEAD,), [None], o, ext, g)
    finish_rows(0, first, o, gain_m, back, up, down, x)
    hs = normed(1, x, gain_a)
    for g in range(2):
        all_project(1, info, temps, hs, wq1, None, kv_out, g)


def last_kernel(
    info, x_ref, q_ref, kv, prior, kv0, gain_m, wo, wu, wd, a, b, d, e,
    out, back, up, down, o, ext, sems,
):
    copies = open_rest(1, info, (wo, wu, wd), (a, b, d, e), back, up, down, sems)
    shuts = [None, shut_if(info[1] < 1), shut_if(info[1] < 2)]
    for g in range(2):
        mine, theirs = g * 2 * HEAD, (1 - g) * 2 * HEAD
        mix(q_ref, (kv, prior, kv0), (mine, theirs, mine), shuts, o, ext, g)
    wait(copies)
    finish_rows(1, x_ref, o, gain_m, back, up, down, out)


def ext_scratch(n):
    return pltpu.VMEM((n, S, 2 * HEAD), BF)


def shards(x, gain_a, wqkv, temps, wout, gain_m, wup, wdown):
    me = lax.axis_index(BOTH)
    info = jnp.stack([(me >> 1) & 1, me, me & 1]).astype(jnp.int32)
    x = x[0]
    own = (wout, wup, wdown)
    own_in = [(HBM, w) for w in own]
    p = cut(info, (wqkv, *own))
    first, mark = spread_first(x)
    q0 = fetch(p[0:2])
    r0 = fetch(p[2:4], (mark, q0[1]))
    q1 = fetch(p[4:6], r0[1])
    r1 = fetch(p[6:8], q1[1])
    q0, r0, q1 = swap(q0), swap(r0), swap(q1)
    sems = pltpu.SemaphoreType.DMA((15,))

    head = [(SMEM, info), (SMEM, temps)]
    q, kv, wq0 = call(
        qkv_kernel,
        "qkv",
        [Q, KV, WQ],
        head + [(VMEM, x), (VMEM, gain_a), (HBM, wqkv)] + [(HBM, w) for w in q0],
        4 * S * D * G,
        [sems],
    )
    prior = send(kv, NEXT)
    back, up, down = call(
        functools.partial(prepare_kernel, 0),
        "prepare",
        REST,
        [(SMEM, info)] + own_in + [(HBM, w) for w in r0],
        0,
        [sems],
    )
    acc, top = call(
        begin_kernel,
        "begin",
        [jax.ShapeDtypeStruct((2 * RATIO * S, w), F32) for w in (2 * HEAD, HEAD)],
        [(SMEM, info), (VMEM, q), (VMEM, kv), (VMEM, prior)],
        8 * S * S * D,
        [ext_scratch(2)],
    )
    weights = [(VMEM, w) for w in (wq0, back, up, down)]
    gains = [(VMEM, gain_a), (VMEM, gain_m)]
    x, q, kv, kv0, wq1 = call(
        own_kernel,
        "own",
        [X, Q, KV, KV, WQ],
        head
        + [(VMEM, v) for v in (first, x, q, acc, top)]
        + gains
        + weights
        + [(HBM, wqkv)]
        + [(HBM, w) for w in q1],
        14 * S * D * D + 4 * S * S * D,
        [pltpu.VMEM((S, D), BF), ext_scratch(1), sems],
    )
    prior = send(kv, NEXT)
    r1 = swap(r1, kv)
    (kv0,) = call(
        first_kernel,
        "first",
        [KV],
        head
        + [(VMEM, first), (VMEM, kv0)]
        + gains
        + weights
        + [(VMEM, wq1)],
        14 * S * D * D + 4 * S * S * D,
        [pltpu.VMEM(Q.shape, BF)] + [pltpu.VMEM((S, D), BF)] * 2 + [ext_scratch(1)],
    )
    (x,) = call(
        last_kernel,
        "last",
        [X],
        [(SMEM, info)]
        + [(VMEM, v) for v in (x, q, kv, prior, kv0, gain_m)]
        + own_in
        + [(HBM, w) for w in r1],
        10 * S * D * D + 12 * S * S * D,
        [pltpu.VMEM(w.shape, BF) for w in REST] + [pltpu.VMEM((S, D), BF), ext_scratch(3), sems],
    )
    return x[None]


def solution(mesh):
    in_specs = (
        P(BOTH, None, None),
        P(),
        P(None, None, "mp"),
        P(),
        P(None, "mp", None),
        P(),
        P(None, None, "mp"),
        P(None, "mp", None),
    )
    return jax.shard_map(
        shards, mesh=mesh, in_specs=in_specs, out_specs=P(BOTH, None, None), check_vma=False
    )
```

```python
import functools
import math

import jax
import jax.numpy as jnp
from jax import lax
from jax.experimental import pallas as pl
from jax.experimental.pallas import tpu as pltpu
from jax.sharding import PartitionSpec as P

HEAD = 128
RATIO = 3
S = 384
D = 768
G = (RATIO + 2) * HEAD
BOTH = ("tm", "mp")
COUNT = 256
BF = jnp.bfloat16
F32 = jnp.float32
QSCALE = 1.0 / (math.sqrt(HEAD) * math.log(2.0))


def place(i):
    return (i >> 7) * 2 + (i & 1), (i >> 2) & 3, (i >> 4) & 7, (i >> 1) & 1


def index(x, y, z, c):
    return ((x >> 1) << 7) | (z << 4) | (y << 2) | (c << 1) | (x & 1)


def pairs(fn):
    return [(i, index(*fn(*place(i)))) for i in range(COUNT)]


def zodd(z):
    return ((((z + 1) & 7) ^ 1) - 1) & 7


X1 = pairs(lambda x, y, z, c: (x ^ 1, y, z, c))
X3 = pairs(lambda x, y, z, c: (x ^ 3, y, z, c))
Y1 = pairs(lambda x, y, z, c: (x, y ^ 1, z, c))
Y3 = pairs(lambda x, y, z, c: (x, y ^ 3, z, c))
Z1 = pairs(lambda x, y, z, c: (x, y, z ^ 1, c))
Z2 = pairs(lambda x, y, z, c: (x, y, z ^ 2, c))
Z6 = pairs(lambda x, y, z, c: (x, y, (((z + 2) & 7) ^ 2) - 2 & 7, c))
CORE = pairs(lambda x, y, z, c: (x, y, z, 1 - c))
NEXT = [(i, i + 1) for i in range(COUNT - 1)]


def send(v, p):
    return lax.ppermute(v, BOTH, p)


def spread_first(x, p, joint):
    me = lax.axis_index(BOTH)
    px, py, pz, pc = (me >> 7) * 2 + (me & 1), (me >> 2) & 3, (me >> 4) & 7, (me >> 1) & 1
    half = D // 2
    got = send(x[:, half:], CORE)
    cur = jnp.where(pc == 0, x[:, :half], got)
    cur, p = lax.optimization_barrier((cur, p))
    q0 = fetch(p[0:2])
    cur = jnp.where(py == 0, cur[:192], send(cur[192:], Y3))
    cur = jnp.where((py == 0) | (py == 3), cur[:96], send(cur[96:], Y1))
    cur = jnp.where(pz == 0, cur[:48], send(cur[48:], Z1))
    cur, q0 = lax.optimization_barrier((cur, q0))
    cur = jnp.where(px == 0, cur, send(cur, X1))
    q0 = swap(q0)
    cur = jnp.where(px < 2, cur, send(cur, X3))
    early = cur
    q, kv, wq = joint(0, x, q0)
    prior = send(kv, NEXT)
    a, b = send(cur, Z2), send(cur, Z6)
    cur = jnp.where(pz < 2, cur, jnp.where(pz < 4, a, b))
    got = send(cur, Z6)
    cur = jnp.where((pz == 4) | (pz == 5), got, cur)
    cur, kv = lax.optimization_barrier((cur, kv))
    cur = jnp.concatenate([cur, send(cur, Z1)], axis=0)
    cur = jnp.concatenate([cur, send(cur, Y1)], axis=0)
    cur = jnp.concatenate([cur, send(cur, Y3)], axis=0)
    cur, prior = lax.optimization_barrier((cur, prior))
    got = send(cur, CORE)
    whole = jnp.where(
        pc == 0, jnp.concatenate([cur, got], axis=1), jnp.concatenate([got, cur], axis=1)
    )
    return whole, early, p, (q, kv, wq, prior)


VMEM = pl.BlockSpec(memory_space=pltpu.VMEM)
SMEM = pl.BlockSpec(memory_space=pltpu.SMEM)
ANY = pl.BlockSpec(memory_space=pl.ANY)
HBM = pl.BlockSpec(memory_space=pltpu.HBM)
NQ, NO, NU = 192, 96, 192
ROWS = NO + 2 * NU


def params(mib=40):
    return pltpu.CompilerParams(vmem_limit_bytes=mib << 20)


def cost(flops, nbytes):
    return pl.CostEstimate(flops=flops, bytes_accessed=nbytes, transcendentals=0)


def cut_kernel(info, wq, wo, wu, wd, *refs):
    outs, stage_q, stage_r, sems = refs[:8], refs[8], refs[9], refs[10]
    core = info[0]
    loads = []
    for l in range(2):
        for j in range(2):
            at = 0
            for i, (src, n) in enumerate(((wq, NQ), (wo, NO), (wu, NU), (wd, NU))):
                rows = pl.ds(pl.multiple_of(core * (2 * n) + j * n, 16), n)
                if i == 0:
                    to = stage_q.at[2 * l + j]
                else:
                    to = stage_r.at[2 * l + j, pl.ds(at, n)]
                    at += n
                loads.append(bring(src.at[l, rows], to, sems.at[8 * l + 4 * j + i]))
    stores = []
    for l in range(2):
        for j in range(2):
            k = 2 * l + j
            loads[4 * k].wait()
            stores.append(bring(stage_q.at[k], outs[4 * l + j], sems.at[16 + 2 * k]))
            wait(loads[4 * k + 1 : 4 * k + 4])
            stores.append(bring(stage_r.at[k], outs[4 * l + 2 + j], sems.at[17 + 2 * k]))
    wait(stores)


def cut(info, weights):
    shapes = ([jax.ShapeDtypeStruct((NQ, G), BF)] * 2 + [jax.ShapeDtypeStruct((ROWS, D), BF)] * 2) * 2
    return pl.pallas_call(
        cut_kernel,
        out_shape=shapes,
        in_specs=[SMEM] + [HBM] * 4,
        out_specs=[HBM] * 8,
        scratch_shapes=[
            pltpu.VMEM((4, NQ, G), BF),
            pltpu.VMEM((4, ROWS, D), BF),
            pltpu.SemaphoreType.DMA((24,)),
        ],
        compiler_params=params(63),
        name="cut",
    )(info, *weights)


def fetch(p, after=None):
    if after is not None:
        p, _ = lax.optimization_barrier((p, after))
    return send(p[0], X1), send(p[1], X3)


def swap(ab, after=None):
    if after is not None:
        ab, _ = lax.optimization_barrier((ab, after))
    return *ab, send(ab[0], CORE), send(ab[1], CORE)


def fill(info, quarters, at, n, dst, base, sems, first):
    width = dst.shape[1]
    copies = []
    for j, ref in enumerate(quarters):
        who = info[0] if j < 2 else 1 - info[0]
        row = pl.multiple_of(base + who * (2 * n) + (j % 2) * n, 16)
        c = pltpu.make_async_copy(
            ref.at[pl.ds(at, n), pl.ds(0, width)], dst.at[pl.ds(row, n)], sems.at[first + j]
        )
        c.start()
        copies.append(c)
    return copies


def bring(src, dst, sem):
    c = pltpu.make_async_copy(src, dst, sem)
    c.start()
    return c


def wait(copies):
    for c in copies:
        c.wait()


def rms(t, gain):
    scale = lax.rsqrt(jnp.mean(t * t, axis=-1, keepdims=True) + 1e-06)
    return (t * scale * gain).astype(BF)


def dot(a, b):
    return jnp.dot(a, b, preferred_element_type=F32)


def dot_t(a, b):
    return lax.dot_general(a, b, (((1,), (1,)), ((), ())), preferred_element_type=F32)


def head_norm(t):
    return t * lax.rsqrt(jnp.mean(t * t, axis=-1, keepdims=True) + 1e-06)


def open_qkv(l, info, wq, quarters, w, sems):
    return [bring(wq.at[l], w.at[pl.ds(0, D)], sems.at[4])] + fill(
        info, quarters, 0, NQ, w, D, sems, 0
    )


def open_rest(l, info, own, quarters, back, up, down, sems):
    wo, wu, wd = own
    copies = [bring(wo.at[l], back.at[pl.ds(0, S)], sems.at[12])]
    copies += fill(info, quarters, 0, NO, back, S, sems, 0)
    copies += [bring(wu.at[l], up.at[pl.ds(0, D)], sems.at[13])]
    copies += fill(info, quarters, NO, NU, up, D, sems, 4)
    copies += [bring(wd.at[l], down.at[pl.ds(0, D)], sems.at[14])]
    copies += fill(info, quarters, NO + NU, NU, down, D, sems, 8)
    return copies


def scales(info, temps, l, g):
    group = info[2] if g == 0 else 1 - info[2]
    return [temps[l, group * RATIO + r] * QSCALE for r in range(RATIO)]


def project(h, w, ts, q_ref, kv_ref, row, g, keys):
    n = h.shape[0]
    first = 0 if ts is not None else RATIO * HEAD
    last = G if keys else RATIO * HEAD
    raw = dot(h, w[pl.ds(g * D, D), first:last])
    if ts is not None:
        for r in range(RATIO):
            t = head_norm(raw[:, r * HEAD : (r + 1) * HEAD])
            q_ref[pl.ds((g * RATIO + r) * S + row, n), :] = (t * ts[r]).astype(BF)
    if keys:
        at = RATIO * HEAD - first
        kv_ref[pl.ds(row, n), pl.ds(g * 2 * HEAD, HEAD)] = head_norm(
            raw[:, at : at + HEAD]
        ).astype(BF)
        kv_ref[pl.ds(row, n), pl.ds(g * 2 * HEAD + HEAD, HEAD)] = raw[:, at + HEAD :].astype(BF)


QKV_STEP = 192
MIX_STEP = 192
END_STEP = 192
WQ = jax.ShapeDtypeStruct((2 * D, G), BF)
REST = [jax.ShapeDtypeStruct((n * D, D), BF) for n in (1, 2, 2)]
KV = jax.ShapeDtypeStruct((S, 4 * HEAD), BF)
Q = jax.ShapeDtypeStruct((2 * RATIO * S, HEAD), BF)
X = jax.ShapeDtypeStruct((S, D), BF)


def normed(l, x_ref, gain):
    return [
        rms(x_ref[pl.ds(row, QKV_STEP), :].astype(F32), gain[pl.ds(l, 1), :])
        for row in range(0, S, QKV_STEP)
    ]


def all_project(l, info, temps, hs, w, q_ref, kv_ref, g):
    ts = None if q_ref is None else scales(info, temps, l, g)
    for i, h in enumerate(hs):
        project(h, w, ts, q_ref, kv_ref, i * QKV_STEP, g, kv_ref is not None)


def call(body, name, outs, ins, flops, scratch=()):
    return pl.pallas_call(
        body,
        out_shape=outs,
        in_specs=[spec for spec, _ in ins],
        out_specs=[VMEM] * len(outs),
        scratch_shapes=list(scratch),
        compiler_params=params(16),
        cost_estimate=cost(flops, 8 << 20),
        name=name,
    )(*[v for _, v in ins])


def qkv_kernel(l, info, temps, x_ref, gain, wq, a, b, d, e, q_ref, kv_ref, w, sems):
    copies = open_qkv(l, info, wq, (a, b, d, e), w, sems)
    copies[0].wait()
    hs = normed(l, x_ref, gain)
    all_project(l, info, temps, hs, w, q_ref, kv_ref, 0)
    wait(copies[1:])
    all_project(l, info, temps, hs, w, q_ref, kv_ref, 1)


def spread_values(kv, at, ext, i):
    ext[i, :, :HEAD] = kv[:, at + HEAD : at + 2 * HEAD]
    ext[i, :, HEAD:] = jnp.ones((S, HEAD), BF)


def blocks():
    return [(r, row) for r in range(RATIO) for row in range(0, S, MIX_STEP)]


def soften(q, kvs, columns, shuts, ext, old=None):
    scores = [dot_t(q, kv[:, at : at + HEAD]) for kv, at in zip(kvs, columns)]
    top = None if old is None else old[1]
    for s, shut in zip(scores, shuts):
        t = s.max(axis=-1, keepdims=True)
        t = t if shut is None else t - shut
        top = t if top is None else jnp.maximum(top, t)
    acc = None if old is None else old[0] * jnp.exp2(old[1] - top)
    for i, (s, shut) in enumerate(zip(scores, shuts)):
        base = top if shut is None else top + shut
        part = dot(jnp.exp2(s - base).astype(BF), ext[i])
        acc = part if acc is None else acc + part
    return acc, top


def close(acc):
    return (acc[:, :HEAD] / acc[:, HEAD:]).astype(BF)


def mix(q_ref, kvs, columns, shuts, o_ref, ext, g):
    for i, (kv, at) in enumerate(zip(kvs, columns)):
        spread_values(kv, at, ext, i)
    for r, row in blocks():
        h = g * RATIO + r
        acc, _ = soften(q_ref[pl.ds(h * S + row, MIX_STEP), :], kvs, columns, shuts, ext)
        o_ref[pl.ds(row, MIX_STEP), pl.ds(h * HEAD, HEAD)] = close(acc)


def shut_if(bad):
    return jnp.where(bad, 1e30, 0.0)


def begin_kernel(info, q_ref, kv, prior, acc_ref, top_ref, ext):
    shuts = [None, shut_if(info[1] < 1)]
    for g in range(2):
        columns = (g * 2 * HEAD, (1 - g) * 2 * HEAD)
        for i, (v, at) in enumerate(zip((kv, prior), columns)):
            spread_values(v, at, ext, i)
        for r, row in blocks():
            rows = pl.ds((g * RATIO + r) * S + row, MIX_STEP)
            acc, top = soften(q_ref[rows, :], (kv, prior), columns, shuts, ext)
            acc_ref[rows, :] = acc
            top_ref[rows, :] = jnp.broadcast_to(top, (MIX_STEP, HEAD))


def finish_rows(l, x_ref, o_ref, gain, back, up, down, out):
    for row in range(0, S, END_STEP):
        rows = pl.ds(row, END_STEP)
        x = (x_ref[rows, :].astype(F32) + dot(o_ref[rows, :], back[...])).astype(BF)
        h = rms(x.astype(F32), gain[pl.ds(l, 1), :])
        y = x.astype(F32)
        for g in range(2):
            t = jax.nn.gelu(dot(h, up[pl.ds(g * D, D), :]), approximate=True).astype(BF)
            y = y + dot(t, down[pl.ds(g * D, D), :])
        out[rows, :] = y.astype(BF)


def own_kernel(
    info, temps, first, x_ref, q_ref, acc_ref, top_ref, gain_a, gain_m, wq0,
    wo, wu, wd, a, b, d, e, out, kv0, back, up, down, o, ext, sems,
):
    copies = open_rest(0, info, (wo, wu, wd), (a, b, d, e), back, up, down, sems)
    hs = normed(0, first, gain_a)
    shuts = [shut_if(info[1] < 2)]
    for g in range(2):
        all_project(0, info, temps, hs, wq0, None, kv0, g)
        at = g * 2 * HEAD
        spread_values(kv0, at, ext, 0)
        for r, row in blocks():
            h = g * RATIO + r
            rows = pl.ds(h * S + row, MIX_STEP)
            old = (acc_ref[rows, :], top_ref[rows, :1])
            acc, _ = soften(q_ref[rows, :], (kv0,), (at,), shuts, ext, old)
            o[pl.ds(row, MIX_STEP), pl.ds(h * HEAD, HEAD)] = close(acc)
    wait(copies)
    finish_rows(0, x_ref, o, gain_m, back, up, down, out)


def first_kernel(
    info, temps, first, kv0, gain_a, gain_m, wq0, back, up, down, wq1,
    kv_out, q, o, x, ext,
):
    hs = normed(0, first, gain_a)
    for g in range(2):
        all_project(0, info, temps, hs, wq0, q, None, g)
        mix(q, (kv0,), (g * 2 * HEAD,), [None], o, ext, g)
    finish_rows(0, first, o, gain_m, back, up, down, x)
    hs = normed(1, x, gain_a)
    for g in range(2):
        all_project(1, info, temps, hs, wq1, None, kv_out, g)


def last_kernel(
    info, x_ref, q_ref, kv, prior, kv0, gain_m, wo, wu, wd, a, b, d, e,
    out, back, up, down, o, ext, sems,
):
    copies = open_rest(1, info, (wo, wu, wd), (a, b, d, e), back, up, down, sems)
    shuts = [None, shut_if(info[1] < 1), shut_if(info[1] < 2)]
    for g in range(2):
        mine, theirs = g * 2 * HEAD, (1 - g) * 2 * HEAD
        mix(q_ref, (kv, prior, kv0), (mine, theirs, mine), shuts, o, ext, g)
    wait(copies)
    finish_rows(1, x_ref, o, gain_m, back, up, down, out)


def ext_scratch(n):
    return pltpu.VMEM((n, S, 2 * HEAD), BF)


def shards(x, gain_a, wqkv, temps, wout, gain_m, wup, wdown):
    me = lax.axis_index(BOTH)
    info = jnp.stack([(me >> 1) & 1, me, me & 1]).astype(jnp.int32)
    x = x[0]
    own = (wout, wup, wdown)
    own_in = [(HBM, w) for w in own]
    sems = pltpu.SemaphoreType.DMA((15,))
    head = [(SMEM, info), (SMEM, temps)]

    def joint(l, x, quarters):
        return call(
            functools.partial(qkv_kernel, l),
            "qkv",
            [Q, KV, WQ],
            head + [(VMEM, x), (VMEM, gain_a), (HBM, wqkv)] + [(HBM, w) for w in quarters],
            4 * S * D * G,
            [sems],
        )

    first, early, p, made = spread_first(x, cut(info, (wqkv, *own)), joint)
    q, kv, wq0, prior = made
    r0 = fetch(p[2:4], early)
    q1 = fetch(p[4:6], kv)
    r0 = swap(r0)
    prior, q1 = lax.optimization_barrier((prior, q1))
    acc, top = call(
        begin_kernel,
        "begin",
        [jax.ShapeDtypeStruct((2 * RATIO * S, w), F32) for w in (2 * HEAD, HEAD)],
        [(SMEM, info), (VMEM, q), (VMEM, kv), (VMEM, prior)],
        8 * S * S * D,
        [ext_scratch(2)],
    )
    r1 = fetch(p[6:8], acc)
    gains = [(VMEM, gain_a), (VMEM, gain_m)]
    x, kv0, back, up, down = call(
        own_kernel,
        "own",
        [X, KV] + REST,
        head
        + [(VMEM, v) for v in (first, x, q, acc, top)]
        + gains
        + [(VMEM, wq0)]
        + own_in
        + [(HBM, w) for w in r0],
        14 * S * D * D + 4 * S * S * D,
        [pltpu.VMEM((S, D), BF), ext_scratch(1), sems],
    )
    q, kv, wq1 = joint(1, x, swap(q1, acc))
    prior = send(kv, NEXT)
    weights = [(VMEM, w) for w in (wq0, back, up, down)]
    r1 = swap(r1, kv)
    (kv0,) = call(
        first_kernel,
        "first",
        [KV],
        head
        + [(VMEM, first), (VMEM, kv0)]
        + gains
        + weights
        + [(VMEM, wq1)],
        14 * S * D * D + 4 * S * S * D,
        [pltpu.VMEM(Q.shape, BF)] + [pltpu.VMEM((S, D), BF)] * 2 + [ext_scratch(1)],
    )
    (x,) = call(
        last_kernel,
        "last",
        [X],
        [(SMEM, info)]
        + [(VMEM, v) for v in (x, q, kv, prior, kv0, gain_m)]
        + own_in
        + [(HBM, w) for w in r1],
        10 * S * D * D + 12 * S * S * D,
        [pltpu.VMEM(w.shape, BF) for w in REST] + [pltpu.VMEM((S, D), BF), ext_scratch(3), sems],
    )
    return x[None]


def solution(mesh):
    in_specs = (
        P(BOTH, None, None),
        P(),
        P(None, None, "mp"),
        P(),
        P(None, "mp", None),
        P(),
        P(None, None, "mp"),
        P(None, "mp", None),
    )
    return jax.shard_map(
        shards, mesh=mesh, in_specs=in_specs, out_specs=P(BOTH, None, None), check_vma=False
    )
```

```python
import functools
import math

import jax
import jax.numpy as jnp
from jax import lax
from jax.experimental import pallas as pl
from jax.experimental.pallas import tpu as pltpu
from jax.sharding import PartitionSpec as P

HEAD = 128
RATIO = 3
S = 384
D = 768
G = (RATIO + 2) * HEAD
BOTH = ("tm", "mp")
COUNT = 256
BF = jnp.bfloat16
F32 = jnp.float32
QSCALE = 1.0 / (math.sqrt(HEAD) * math.log(2.0))


def place(i):
    return (i >> 7) * 2 + (i & 1), (i >> 2) & 3, (i >> 4) & 7, (i >> 1) & 1


def index(x, y, z, c):
    return ((x >> 1) << 7) | (z << 4) | (y << 2) | (c << 1) | (x & 1)


def pairs(fn):
    return [(i, index(*fn(*place(i)))) for i in range(COUNT)]


def zodd(z):
    return ((((z + 1) & 7) ^ 1) - 1) & 7


X1 = pairs(lambda x, y, z, c: (x ^ 1, y, z, c))
X3 = pairs(lambda x, y, z, c: (x ^ 3, y, z, c))
Y1 = pairs(lambda x, y, z, c: (x, y ^ 1, z, c))
Y3 = pairs(lambda x, y, z, c: (x, y ^ 3, z, c))
Z1 = pairs(lambda x, y, z, c: (x, y, z ^ 1, c))
Z2 = pairs(lambda x, y, z, c: (x, y, z ^ 2, c))
Z6 = pairs(lambda x, y, z, c: (x, y, (((z + 2) & 7) ^ 2) - 2 & 7, c))
CORE = pairs(lambda x, y, z, c: (x, y, z, 1 - c))
NEXT = [(i, i + 1) for i in range(COUNT - 1)]


def send(v, p):
    return lax.ppermute(v, BOTH, p)


def spread_first(x, pq, rest, joint):
    me = lax.axis_index(BOTH)
    px, py, pz, pc = (me >> 7) * 2 + (me & 1), (me >> 2) & 3, (me >> 4) & 7, (me >> 1) & 1
    tie = lax.optimization_barrier
    half = D // 2
    got = send(x[:, half:], CORE)
    cur = jnp.where(pc == 0, x[:, :half], got)
    cur, pq = tie((cur, pq))
    q0 = fetch(pq)
    cur = jnp.where(py == 0, cur[:192], send(cur[192:], Y3))
    pr, pq1, pr1 = rest(cur)
    cur, pr, pq1, pr1 = tie((cur, pr, pq1, pr1))
    cur = jnp.where((py == 0) | (py == 3), cur[:96], send(cur[96:], Y1))
    cur, q0 = tie((cur, q0))
    q0 = swap(q0)
    cur = jnp.where(pz == 0, cur[:48], send(cur[48:], Z1))
    cur = jnp.where(px == 0, cur, send(cur, X1))
    cur, q0 = tie((cur, q0))
    q, kv, wq = joint(0, x, q0)
    cur = jnp.where(px < 2, cur, send(cur, X3))
    cur, kv = tie((cur, kv))
    prior = send(kv, NEXT)
    r0 = fetch(pr, cur)
    a, b = send(cur, Z2), send(cur, Z6)
    cur = jnp.where(pz < 2, cur, jnp.where(pz < 4, a, b))
    got = send(cur, Z6)
    cur = jnp.where((pz == 4) | (pz == 5), got, cur)
    cur = jnp.concatenate([cur, send(cur, Z1)], axis=0)
    q1 = fetch(pq1, cur)
    cur = jnp.concatenate([cur, send(cur, Y1)], axis=0)
    cur, prior = tie((cur, prior))
    cur = jnp.concatenate([cur, send(cur, Y3)], axis=0)
    got = send(cur, CORE)
    whole = jnp.where(
        pc == 0, jnp.concatenate([cur, got], axis=1), jnp.concatenate([got, cur], axis=1)
    )
    whole, q1 = tie((whole, q1))
    return whole, q, kv, wq, prior, r0, q1, pr1


VMEM = pl.BlockSpec(memory_space=pltpu.VMEM)
SMEM = pl.BlockSpec(memory_space=pltpu.SMEM)
ANY = pl.BlockSpec(memory_space=pl.ANY)
HBM = pl.BlockSpec(memory_space=pltpu.HBM)
NQ, NO, NU = 192, 96, 192
ROWS = NO + 2 * NU


def params(mib=40):
    return pltpu.CompilerParams(vmem_limit_bytes=mib << 20)


def cost(flops, nbytes):
    return pl.CostEstimate(flops=flops, bytes_accessed=nbytes, transcendentals=0)


def cut_kernel(parts, info, *refs):
    k = 1 + max(i for part in parts for i, _, _ in part)
    n = len(parts)
    sources, outs, stages, sems = refs[:k], refs[k : k + 2 * n], refs[k + 2 * n : -1], refs[-1]
    core = info[0]
    at = 0
    loads = []
    for stage, part in zip(stages, parts):
        for j in range(2):
            to = 0
            group = []
            for i, l, rows in part:
                row = pl.multiple_of(core * (2 * rows) + j * rows, 16)
                group.append(
                    bring(
                        sources[i].at[l, pl.ds(row, rows)],
                        stage.at[j, pl.ds(to, rows)],
                        sems.at[at],
                    )
                )
                to += rows
                at += 1
            loads.append(group)
    stores = []
    for m, group in enumerate(loads):
        wait(group)
        stores.append(bring(stages[m // 2].at[m % 2], outs[m], sems.at[at]))
        at += 1
    wait(stores)


def cut(info, sources, parts):
    widths = [sources[part[0][0]].shape[2] for part in parts]
    heights = [sum(rows for _, _, rows in part) for part in parts]
    shapes = []
    for n, w in zip(heights, widths):
        shapes += [jax.ShapeDtypeStruct((n, w), BF)] * 2
    flat = pl.pallas_call(
        functools.partial(cut_kernel, parts),
        out_shape=shapes,
        in_specs=[SMEM] + [HBM] * len(sources),
        out_specs=[HBM] * len(shapes),
        scratch_shapes=[pltpu.VMEM((2, n, w), BF) for n, w in zip(heights, widths)]
        + [pltpu.SemaphoreType.DMA((2 * sum(len(part) + 1 for part in parts),))],
        compiler_params=params(63),
        name="cut",
    )(info, *sources)
    return [flat[2 * i : 2 * i + 2] for i in range(len(parts))]


def fetch(p, after=None):
    if after is not None:
        p, _ = lax.optimization_barrier((p, after))
    return send(p[0], X1), send(p[1], X3)


def swap(ab, after=None):
    if after is not None:
        ab, _ = lax.optimization_barrier((ab, after))
    return *ab, send(ab[0], CORE), send(ab[1], CORE)


def fill(info, quarters, at, n, dst, base, sems, first):
    width = dst.shape[1]
    copies = []
    for j, ref in enumerate(quarters):
        who = info[0] if j < 2 else 1 - info[0]
        row = pl.multiple_of(base + who * (2 * n) + (j % 2) * n, 16)
        c = pltpu.make_async_copy(
            ref.at[pl.ds(at, n), pl.ds(0, width)], dst.at[pl.ds(row, n)], sems.at[first + j]
        )
        c.start()
        copies.append(c)
    return copies


def bring(src, dst, sem):
    c = pltpu.make_async_copy(src, dst, sem)
    c.start()
    return c


def wait(copies):
    for c in copies:
        c.wait()


def rms(t, gain):
    scale = lax.rsqrt(jnp.mean(t * t, axis=-1, keepdims=True) + 1e-06)
    return (t * scale * gain).astype(BF)


def dot(a, b):
    return jnp.dot(a, b, preferred_element_type=F32)


def dot_t(a, b):
    return lax.dot_general(a, b, (((1,), (1,)), ((), ())), preferred_element_type=F32)


def head_norm(t):
    return t * lax.rsqrt(jnp.mean(t * t, axis=-1, keepdims=True) + 1e-06)


def open_qkv(l, info, wq, quarters, w, sems):
    return [bring(wq.at[l], w.at[pl.ds(0, D)], sems.at[4])] + fill(
        info, quarters, 0, NQ, w, D, sems, 0
    )


def open_rest(l, info, own, quarters, back, up, down, sems):
    wo, wu, wd = own
    copies = [bring(wo.at[l], back.at[pl.ds(0, S)], sems.at[12])]
    copies += fill(info, quarters, 0, NO, back, S, sems, 0)
    copies += [bring(wu.at[l], up.at[pl.ds(0, D)], sems.at[13])]
    copies += fill(info, quarters, NO, NU, up, D, sems, 4)
    copies += [bring(wd.at[l], down.at[pl.ds(0, D)], sems.at[14])]
    copies += fill(info, quarters, NO + NU, NU, down, D, sems, 8)
    return copies


def scales(info, temps, l, g):
    group = info[2] if g == 0 else 1 - info[2]
    return [temps[l, group * RATIO + r] * QSCALE for r in range(RATIO)]


def project(h, w, ts, q_ref, kv_ref, row, g, keys):
    n = h.shape[0]
    first = 0 if ts is not None else RATIO * HEAD
    last = G if keys else RATIO * HEAD
    raw = dot(h, w[pl.ds(g * D, D), first:last])
    if ts is not None:
        for r in range(RATIO):
            t = head_norm(raw[:, r * HEAD : (r + 1) * HEAD])
            q_ref[pl.ds((g * RATIO + r) * S + row, n), :] = (t * ts[r]).astype(BF)
    if keys:
        at = RATIO * HEAD - first
        kv_ref[pl.ds(row, n), pl.ds(g * 2 * HEAD, HEAD)] = head_norm(
            raw[:, at : at + HEAD]
        ).astype(BF)
        kv_ref[pl.ds(row, n), pl.ds(g * 2 * HEAD + HEAD, HEAD)] = raw[:, at + HEAD :].astype(BF)


QKV_STEP = 192
MIX_STEP = 192
END_STEP = 192
WQ = jax.ShapeDtypeStruct((2 * D, G), BF)
REST = [jax.ShapeDtypeStruct((n * D, D), BF) for n in (1, 2, 2)]
KV = jax.ShapeDtypeStruct((S, 4 * HEAD), BF)
Q = jax.ShapeDtypeStruct((2 * RATIO * S, HEAD), BF)
X = jax.ShapeDtypeStruct((S, D), BF)


def over(n, step, body):
    @pl.loop(0, n // step)
    def _(i):
        body(pl.multiple_of(i * step, step))


def norm_all(l, x_ref, gain, h):
    def one(row):
        rows = pl.ds(row, QKV_STEP)
        h[rows, :] = rms(x_ref[rows, :].astype(F32), gain[pl.ds(l, 1), :])

    over(S, QKV_STEP, one)


def all_project(l, info, temps, h, w, q_ref, kv_ref, g):
    ts = None if q_ref is None else scales(info, temps, l, g)

    def one(row):
        project(h[pl.ds(row, QKV_STEP), :], w, ts, q_ref, kv_ref, row, g, kv_ref is not None)

    over(S, QKV_STEP, one)


def call(body, name, outs, ins, flops, scratch=()):
    return pl.pallas_call(
        body,
        out_shape=outs,
        in_specs=[spec for spec, _ in ins],
        out_specs=[VMEM] * len(outs),
        scratch_shapes=list(scratch),
        compiler_params=params(16),
        cost_estimate=cost(flops, 8 << 20),
        name=name,
    )(*[v for _, v in ins])


def qkv_kernel(l, info, temps, x_ref, gain, wq, a, b, d, e, q_ref, kv_ref, w, h, sems):
    copies = open_qkv(l, info, wq, (a, b, d, e), w, sems)
    norm_all(l, x_ref, gain, h)
    copies[0].wait()
    all_project(l, info, temps, h, w, q_ref, kv_ref, 0)
    wait(copies[1:])
    all_project(l, info, temps, h, w, q_ref, kv_ref, 1)


def spread_values(kv, at, ext, i):
    ext[i, :, :HEAD] = kv[:, at + HEAD : at + 2 * HEAD]
    ext[i, :, HEAD:] = jnp.ones((S, HEAD), BF)


def each_head(g, body):
    @pl.loop(g * RATIO, (g + 1) * RATIO)
    def _(h):
        for row in range(0, S, MIX_STEP):
            body(
                pl.ds(pl.multiple_of(h * S + row, MIX_STEP), MIX_STEP),
                pl.ds(row, MIX_STEP),
                pl.ds(pl.multiple_of(h * HEAD, HEAD), HEAD),
            )


def soften(q, kvs, columns, shuts, ext, old=None):
    scores = [dot_t(q, kv[:, at : at + HEAD]) for kv, at in zip(kvs, columns)]
    top = None if old is None else old[1]
    for s, shut in zip(scores, shuts):
        t = s.max(axis=-1, keepdims=True)
        t = t if shut is None else t - shut
        top = t if top is None else jnp.maximum(top, t)
    acc = None if old is None else old[0] * jnp.exp2(old[1] - top)
    for i, (s, shut) in enumerate(zip(scores, shuts)):
        base = top if shut is None else top + shut
        part = dot(jnp.exp2(s - base).astype(BF), ext[i])
        acc = part if acc is None else acc + part
    return acc, top


def close(acc):
    return (acc[:, :HEAD] / acc[:, HEAD:]).astype(BF)


def mix(q_ref, kvs, columns, shuts, o_ref, ext, g):
    for i, (kv, at) in enumerate(zip(kvs, columns)):
        spread_values(kv, at, ext, i)

    def one(rows, to, lanes):
        acc, _ = soften(q_ref[rows, :], kvs, columns, shuts, ext)
        o_ref[to, lanes] = close(acc)

    each_head(g, one)


def shut_if(bad):
    return jnp.where(bad, 1e30, 0.0)


def begin_kernel(info, q_ref, kv, prior, acc_ref, top_ref, ext):
    shuts = [None, shut_if(info[1] < 1)]
    for g in range(2):
        columns = (g * 2 * HEAD, (1 - g) * 2 * HEAD)
        for i, (v, at) in enumerate(zip((kv, prior), columns)):
            spread_values(v, at, ext, i)

        def one(rows, to, lanes, columns=columns):
            acc, top = soften(q_ref[rows, :], (kv, prior), columns, shuts, ext)
            acc_ref[rows, :] = acc
            top_ref[rows, :] = jnp.broadcast_to(top, (MIX_STEP, HEAD))

        each_head(g, one)


def finish_rows(l, x_ref, o_ref, gain, back, up, down, out):
    def one(row):
        rows = pl.ds(row, END_STEP)
        x = (x_ref[rows, :].astype(F32) + dot(o_ref[rows, :], back[...])).astype(BF)
        h = rms(x.astype(F32), gain[pl.ds(l, 1), :])
        y = x.astype(F32)
        for g in range(2):
            t = jax.nn.gelu(dot(h, up[pl.ds(g * D, D), :]), approximate=True).astype(BF)
            y = y + dot(t, down[pl.ds(g * D, D), :])
        out[rows, :] = y.astype(BF)

    over(S, END_STEP, one)


def own_kernel(
    info, temps, first, x_ref, q_ref, acc_ref, top_ref, gain_a, gain_m, wq0,
    wo, wu, wd, a, b, d, e, out, kv0, back, up, down, o, h, ext, sems,
):
    copies = open_rest(0, info, (wo, wu, wd), (a, b, d, e), back, up, down, sems)
    norm_all(0, first, gain_a, h)
    shuts = [shut_if(info[1] < 2)]
    for g in range(2):
        all_project(0, info, temps, h, wq0, None, kv0, g)
        at = g * 2 * HEAD
        spread_values(kv0, at, ext, 0)

        def one(rows, to, lanes, at=at):
            old = (acc_ref[rows, :], top_ref[rows, :1])
            acc, _ = soften(q_ref[rows, :], (kv0,), (at,), shuts, ext, old)
            o[to, lanes] = close(acc)

        each_head(g, one)
    wait(copies)
    finish_rows(0, x_ref, o, gain_m, back, up, down, out)


def first_kernel(
    info, temps, first, kv0, gain_a, gain_m, wq0, back, up, down, wq1,
    kv_out, q, o, x, h, ext,
):
    norm_all(0, first, gain_a, h)
    for g in range(2):
        all_project(0, info, temps, h, wq0, q, None, g)
        mix(q, (kv0,), (g * 2 * HEAD,), [None], o, ext, g)
    finish_rows(0, first, o, gain_m, back, up, down, x)
    norm_all(1, x, gain_a, h)
    for g in range(2):
        all_project(1, info, temps, h, wq1, None, kv_out, g)


def last_kernel(
    info, x_ref, q_ref, kv, prior, kv0, gain_m, wo, wu, wd, a, b, d, e,
    out, back, up, down, o, ext, sems,
):
    copies = open_rest(1, info, (wo, wu, wd), (a, b, d, e), back, up, down, sems)
    shuts = [None, shut_if(info[1] < 1), shut_if(info[1] < 2)]
    for g in range(2):
        mine, theirs = g * 2 * HEAD, (1 - g) * 2 * HEAD
        mix(q_ref, (kv, prior, kv0), (mine, theirs, mine), shuts, o, ext, g)
    wait(copies)
    finish_rows(1, x_ref, o, gain_m, back, up, down, out)


def ext_scratch(n):
    return pltpu.VMEM((n, S, 2 * HEAD), BF)


def shards(x, gain_a, wqkv, temps, wout, gain_m, wup, wdown):
    me = lax.axis_index(BOTH)
    info = jnp.stack([(me >> 1) & 1, me, me & 1]).astype(jnp.int32)
    x = x[0]
    own = (wout, wup, wdown)
    own_in = [(HBM, w) for w in own]
    sems = pltpu.SemaphoreType.DMA((15,))
    head = [(SMEM, info), (SMEM, temps)]

    def joint(l, x, quarters):
        return call(
            functools.partial(qkv_kernel, l),
            "qkv",
            [Q, KV, WQ],
            head + [(VMEM, x), (VMEM, gain_a), (HBM, wqkv)] + [(HBM, w) for w in quarters],
            4 * S * D * G,
            [pltpu.VMEM((S, D), BF), sems],
        )

    def rest(after):
        parts = [[(0, 1, NQ)]]
        for l in range(2):
            parts.insert(2 * l, [(1, l, NO), (2, l, NU), (3, l, NU)])
        return cut(info, (wqkv, *own), parts)

    (pq,) = cut(info, (wqkv,), [[(0, 0, NQ)]])
    first, q, kv, wq0, prior, r0, q1, pr1 = spread_first(x, pq, rest, joint)
    r0 = swap(r0)
    acc, top = call(
        begin_kernel,
        "begin",
        [jax.ShapeDtypeStruct((2 * RATIO * S, w), F32) for w in (2 * HEAD, HEAD)],
        [(SMEM, info), (VMEM, q), (VMEM, kv), (VMEM, prior)],
        8 * S * S * D,
        [ext_scratch(2)],
    )
    r1 = fetch(pr1, first)
    gains = [(VMEM, gain_a), (VMEM, gain_m)]
    x, kv0, back, up, down = call(
        own_kernel,
        "own",
        [X, KV] + REST,
        head
        + [(VMEM, v) for v in (first, x, q, acc, top)]
        + gains
        + [(VMEM, wq0)]
        + own_in
        + [(HBM, w) for w in r0],
        14 * S * D * D + 4 * S * S * D,
        [pltpu.VMEM((S, D), BF)] * 2 + [ext_scratch(1), sems],
    )
    q, kv, wq1 = joint(1, x, swap(q1, acc))
    prior = send(kv, NEXT)
    weights = [(VMEM, w) for w in (wq0, back, up, down)]
    r1 = swap(r1, kv)
    (kv0,) = call(
        first_kernel,
        "first",
        [KV],
        head
        + [(VMEM, first), (VMEM, kv0)]
        + gains
        + weights
        + [(VMEM, wq1)],
        14 * S * D * D + 4 * S * S * D,
        [pltpu.VMEM(Q.shape, BF)] + [pltpu.VMEM((S, D), BF)] * 3 + [ext_scratch(1)],
    )
    (x,) = call(
        last_kernel,
        "last",
        [X],
        [(SMEM, info)]
        + [(VMEM, v) for v in (x, q, kv, prior, kv0, gain_m)]
        + own_in
        + [(HBM, w) for w in r1],
        10 * S * D * D + 12 * S * S * D,
        [pltpu.VMEM(w.shape, BF) for w in REST] + [pltpu.VMEM((S, D), BF), ext_scratch(3), sems],
    )
    return x[None]


def solution(mesh):
    in_specs = (
        P(BOTH, None, None),
        P(),
        P(None, None, "mp"),
        P(),
        P(None, "mp", None),
        P(),
        P(None, None, "mp"),
        P(None, "mp", None),
    )
    return jax.shard_map(
        shards, mesh=mesh, in_specs=in_specs, out_specs=P(BOTH, None, None), check_vma=False
    )
```

```python
import functools
import math

import jax
import jax.numpy as jnp
from jax import lax
from jax.experimental import pallas as pl
from jax.experimental.pallas import tpu as pltpu
from jax.sharding import PartitionSpec as P

HEAD = 128
RATIO = 3
S = 384
D = 768
G = (RATIO + 2) * HEAD
BOTH = ("tm", "mp")
COUNT = 256
BF = jnp.bfloat16
F32 = jnp.float32
QSCALE = 1.0 / (math.sqrt(HEAD) * math.log(2.0))


def place(i):
    return (i >> 7) * 2 + (i & 1), (i >> 2) & 3, (i >> 4) & 7, (i >> 1) & 1


def index(x, y, z, c):
    return ((x >> 1) << 7) | (z << 4) | (y << 2) | (c << 1) | (x & 1)


def pairs(fn):
    return [(i, index(*fn(*place(i)))) for i in range(COUNT)]


def zodd(z):
    return ((((z + 1) & 7) ^ 1) - 1) & 7


X1 = pairs(lambda x, y, z, c: (x ^ 1, y, z, c))
X3 = pairs(lambda x, y, z, c: (x ^ 3, y, z, c))
Y1 = pairs(lambda x, y, z, c: (x, y ^ 1, z, c))
Y3 = pairs(lambda x, y, z, c: (x, y ^ 3, z, c))
Z1 = pairs(lambda x, y, z, c: (x, y, z ^ 1, c))
Z2 = pairs(lambda x, y, z, c: (x, y, z ^ 2, c))
Z6 = pairs(lambda x, y, z, c: (x, y, (((z + 2) & 7) ^ 2) - 2 & 7, c))
CORE = pairs(lambda x, y, z, c: (x, y, z, 1 - c))
NEXT = [(i, i + 1) for i in range(COUNT - 1)]


def send(v, p):
    return lax.ppermute(v, BOTH, p)


def spread_first(x, p, joint):
    me = lax.axis_index(BOTH)
    px, py, pz, pc = (me >> 7) * 2 + (me & 1), (me >> 2) & 3, (me >> 4) & 7, (me >> 1) & 1
    tie = lax.optimization_barrier
    half = D // 2
    got = send(x[:, half:], CORE)
    cur = jnp.where(pc == 0, x[:, :half], got)
    cur, p = tie((cur, p))
    q0 = fetch(p[0])
    cur = jnp.where(py == 0, cur[:192], send(cur[192:], Y3))
    cur = jnp.where((py == 0) | (py == 3), cur[:96], send(cur[96:], Y1))
    cur, q0 = tie((cur, q0))
    q0 = swap(q0)
    cur = jnp.where(pz == 0, cur[:48], send(cur[48:], Z1))
    cur = jnp.where(px == 0, cur, send(cur, X1))
    cur, q0 = tie((cur, q0))
    q, kv = joint(0, x, q0)
    cur = jnp.where(px < 2, cur, send(cur, X3))
    cur, kv = tie((cur, kv))
    prior = send(kv, NEXT)
    r0 = fetch(p[1], cur)
    a, b = send(cur, Z2), send(cur, Z6)
    cur = jnp.where(pz < 2, cur, jnp.where(pz < 4, a, b))
    got = send(cur, Z6)
    cur = jnp.where((pz == 4) | (pz == 5), got, cur)
    cur = jnp.concatenate([cur, send(cur, Z1)], axis=0)
    q1 = fetch(p[2], kv)
    cur = jnp.concatenate([cur, send(cur, Y1)], axis=0)
    cur = jnp.concatenate([cur, send(cur, Y3)], axis=0)
    cur, prior = tie((cur, prior))
    got = send(cur, CORE)
    whole = jnp.where(
        pc == 0, jnp.concatenate([cur, got], axis=1), jnp.concatenate([got, cur], axis=1)
    )
    return whole, q, kv, prior, q0, r0, q1


VMEM = pl.BlockSpec(memory_space=pltpu.VMEM)
SMEM = pl.BlockSpec(memory_space=pltpu.SMEM)
ANY = pl.BlockSpec(memory_space=pl.ANY)
HBM = pl.BlockSpec(memory_space=pltpu.HBM)
NQ, NO, NU = 192, 96, 192
ROWS = NO + 2 * NU


def params(mib=40):
    return pltpu.CompilerParams(vmem_limit_bytes=mib << 20)


def cost(flops, nbytes):
    return pl.CostEstimate(flops=flops, bytes_accessed=nbytes, transcendentals=0)


def cut_kernel(parts, info, *refs):
    k = 1 + max(i for part in parts for i, _, _ in part)
    n = len(parts)
    sources, outs, stages, sems = refs[:k], refs[k : k + 2 * n], refs[k + 2 * n : -1], refs[-1]
    core = info[0]
    at = 0
    loads = []
    for stage, part in zip(stages, parts):
        for j in range(2):
            to = 0
            group = []
            for i, l, rows in part:
                row = pl.multiple_of(core * (2 * rows) + j * rows, 16)
                group.append(
                    bring(
                        sources[i].at[l, pl.ds(row, rows)],
                        stage.at[j, pl.ds(to, rows)],
                        sems.at[at],
                    )
                )
                to += rows
                at += 1
            loads.append(group)
    stores = []
    for m, group in enumerate(loads):
        wait(group)
        stores.append(bring(stages[m // 2].at[m % 2], outs[m], sems.at[at]))
        at += 1
    wait(stores)


def cut(info, sources, parts):
    widths = [sources[part[0][0]].shape[2] for part in parts]
    heights = [sum(rows for _, _, rows in part) for part in parts]
    shapes = []
    for n, w in zip(heights, widths):
        shapes += [jax.ShapeDtypeStruct((n, w), BF)] * 2
    flat = pl.pallas_call(
        functools.partial(cut_kernel, parts),
        out_shape=shapes,
        in_specs=[SMEM] + [HBM] * len(sources),
        out_specs=[HBM] * len(shapes),
        scratch_shapes=[pltpu.VMEM((2, n, w), BF) for n, w in zip(heights, widths)]
        + [pltpu.SemaphoreType.DMA((2 * sum(len(part) + 1 for part in parts),))],
        compiler_params=params(63),
        name="cut",
    )(info, *sources)
    return [flat[2 * i : 2 * i + 2] for i in range(len(parts))]


def fetch(p, after=None):
    if after is not None:
        p, _ = lax.optimization_barrier((p, after))
    return send(p[0], X1), send(p[1], X3)


def swap(ab, after=None):
    if after is not None:
        ab, _ = lax.optimization_barrier((ab, after))
    return *ab, send(ab[0], CORE), send(ab[1], CORE)


def fill(info, quarters, at, n, dst, base, sems, first):
    width = dst.shape[1]
    copies = []
    for j, ref in enumerate(quarters):
        who = info[0] if j < 2 else 1 - info[0]
        row = pl.multiple_of(base + who * (2 * n) + (j % 2) * n, 16)
        c = pltpu.make_async_copy(
            ref.at[pl.ds(at, n), pl.ds(0, width)], dst.at[pl.ds(row, n)], sems.at[first + j]
        )
        c.start()
        copies.append(c)
    return copies


def bring(src, dst, sem):
    c = pltpu.make_async_copy(src, dst, sem)
    c.start()
    return c


def wait(copies):
    for c in copies:
        c.wait()


def rms(t, gain):
    scale = lax.rsqrt(jnp.mean(t * t, axis=-1, keepdims=True) + 1e-06)
    return (t * scale * gain).astype(BF)


def dot(a, b):
    return jnp.dot(a, b, preferred_element_type=F32)


def dot_t(a, b):
    return lax.dot_general(a, b, (((1,), (1,)), ((), ())), preferred_element_type=F32)


def head_norm(t):
    return t * lax.rsqrt(jnp.mean(t * t, axis=-1, keepdims=True) + 1e-06)


def open_qkv(l, info, wq, quarters, w, sems):
    return [bring(wq.at[l], w.at[pl.ds(0, D)], sems.at[4])] + fill(
        info, quarters, 0, NQ, w, D, sems, 0
    )


def open_rest(l, info, own, quarters, back, up, down, sems):
    wo, wu, wd = own
    copies = [bring(wo.at[l], back.at[pl.ds(0, S)], sems.at[12])]
    copies += fill(info, quarters, 0, NO, back, S, sems, 0)
    copies += [bring(wu.at[l], up.at[pl.ds(0, D)], sems.at[13])]
    copies += fill(info, quarters, NO, NU, up, D, sems, 4)
    copies += [bring(wd.at[l], down.at[pl.ds(0, D)], sems.at[14])]
    copies += fill(info, quarters, NO + NU, NU, down, D, sems, 8)
    return copies


def scales(info, temps, l, g):
    group = info[2] if g == 0 else 1 - info[2]
    return [temps[l, group * RATIO + r] * QSCALE for r in range(RATIO)]


def project(h, w, ts, q_ref, kv_ref, row, g, keys):
    n = h.shape[0]
    first = 0 if ts is not None else RATIO * HEAD
    last = G if keys else RATIO * HEAD
    raw = dot(h, w[pl.ds(g * D, D), first:last])
    if ts is not None:
        for r in range(RATIO):
            t = head_norm(raw[:, r * HEAD : (r + 1) * HEAD])
            q_ref[pl.ds((g * RATIO + r) * S + row, n), :] = (t * ts[r]).astype(BF)
    if keys:
        at = RATIO * HEAD - first
        kv_ref[pl.ds(row, n), pl.ds(g * 2 * HEAD, HEAD)] = head_norm(
            raw[:, at : at + HEAD]
        ).astype(BF)
        kv_ref[pl.ds(row, n), pl.ds(g * 2 * HEAD + HEAD, HEAD)] = raw[:, at + HEAD :].astype(BF)


QKV_STEP = 192
MIX_STEP = 192
END_STEP = 192
WQ = jax.ShapeDtypeStruct((2 * D, G), BF)
REST = [jax.ShapeDtypeStruct((n * D, D), BF) for n in (1, 2, 2)]
KV = jax.ShapeDtypeStruct((S, 4 * HEAD), BF)
Q = jax.ShapeDtypeStruct((2 * RATIO * S, HEAD), BF)
X = jax.ShapeDtypeStruct((S, D), BF)


def over(n, step, body, loop=False):
    if not loop:
        for row in range(0, n, step):
            body(row)
        return

    @pl.loop(0, n // step)
    def _(i):
        body(pl.multiple_of(i * step, step))


def norm_all(l, x_ref, gain, h):
    def one(row):
        rows = pl.ds(row, QKV_STEP)
        h[rows, :] = rms(x_ref[rows, :].astype(F32), gain[pl.ds(l, 1), :])

    over(S, QKV_STEP, one)


def all_project(l, info, temps, h, w, q_ref, kv_ref, g):
    ts = None if q_ref is None else scales(info, temps, l, g)

    def one(row):
        project(h[pl.ds(row, QKV_STEP), :], w, ts, q_ref, kv_ref, row, g, kv_ref is not None)

    over(S, QKV_STEP, one)


def call(body, name, outs, ins, flops, scratch=(), mib=16):
    return pl.pallas_call(
        body,
        out_shape=outs,
        in_specs=[spec for spec, _ in ins],
        out_specs=[VMEM] * len(outs),
        scratch_shapes=list(scratch),
        compiler_params=params(mib),
        cost_estimate=cost(flops, 8 << 20),
        name=name,
    )(*[v for _, v in ins])


def qkv_kernel(l, info, temps, x_ref, gain, wq, a, b, d, e, q_ref, kv_ref, w, h, sems):
    copies = open_qkv(l, info, wq, (a, b, d, e), w, sems)
    norm_all(l, x_ref, gain, h)
    copies[0].wait()
    all_project(l, info, temps, h, w, q_ref, kv_ref, 0)
    wait(copies[1:])
    all_project(l, info, temps, h, w, q_ref, kv_ref, 1)


def spread_values(kv, at, ext, i):
    ext[i, :, :HEAD] = kv[:, at + HEAD : at + 2 * HEAD]
    ext[i, :, HEAD:] = jnp.ones((S, HEAD), BF)


def each_head(g, body, loop):
    def one(h):
        for row in range(0, S, MIX_STEP):
            body(
                pl.ds(pl.multiple_of(h * S + row, MIX_STEP), MIX_STEP),
                pl.ds(row, MIX_STEP),
                pl.ds(pl.multiple_of(h * HEAD, HEAD), HEAD),
            )

    if loop:
        pl.loop(g * RATIO, (g + 1) * RATIO)(one)
    else:
        for h in range(g * RATIO, (g + 1) * RATIO):
            one(h)


def soften(q, kvs, columns, shuts, ext, old=None):
    scores = [dot_t(q, kv[:, at : at + HEAD]) for kv, at in zip(kvs, columns)]
    top = None if old is None else old[1]
    for s, shut in zip(scores, shuts):
        t = s.max(axis=-1, keepdims=True)
        t = t if shut is None else t - shut
        top = t if top is None else jnp.maximum(top, t)
    acc = None if old is None else old[0] * jnp.exp2(old[1] - top)
    for i, (s, shut) in enumerate(zip(scores, shuts)):
        base = top if shut is None else top + shut
        part = dot(jnp.exp2(s - base).astype(BF), ext[i])
        acc = part if acc is None else acc + part
    return acc, top


def close(acc):
    return (acc[:, :HEAD] / acc[:, HEAD:]).astype(BF)


def mix(q_ref, kvs, columns, shuts, o_ref, ext, g):
    for i, (kv, at) in enumerate(zip(kvs, columns)):
        spread_values(kv, at, ext, i)

    def one(rows, to, lanes):
        acc, _ = soften(q_ref[rows, :], kvs, columns, shuts, ext)
        o_ref[to, lanes] = close(acc)

    each_head(g, one, len(kvs) > 1)


def shut_if(bad):
    return jnp.where(bad, 1e30, 0.0)


def begin_kernel(info, q_ref, kv, prior, acc_ref, top_ref, ext):
    shuts = [None, shut_if(info[1] < 1)]
    for g in range(2):
        columns = (g * 2 * HEAD, (1 - g) * 2 * HEAD)
        for i, (v, at) in enumerate(zip((kv, prior), columns)):
            spread_values(v, at, ext, i)

        def one(rows, to, lanes, columns=columns):
            acc, top = soften(q_ref[rows, :], (kv, prior), columns, shuts, ext)
            acc_ref[rows, :] = acc
            top_ref[rows, :] = jnp.broadcast_to(top, (MIX_STEP, HEAD))

        each_head(g, one, True)


def finish_rows(l, x_ref, o_ref, gain, back, up, down, out):
    def one(row):
        rows = pl.ds(row, END_STEP)
        x = (x_ref[rows, :].astype(F32) + dot(o_ref[rows, :], back[...])).astype(BF)
        h = rms(x.astype(F32), gain[pl.ds(l, 1), :])
        y = x.astype(F32)
        for g in range(2):
            t = jax.nn.gelu(dot(h, up[pl.ds(g * D, D), :]), approximate=True).astype(BF)
            y = y + dot(t, down[pl.ds(g * D, D), :])
        out[rows, :] = y.astype(BF)

    over(S, END_STEP, one, True)


def own_kernel(
    info, temps, first, x_ref, q_ref, acc_ref, top_ref, gain_a, gain_m, wq_ref,
    qa, qb, qd, qe, wo, wu, wd, a, b, d, e, out, kv0, wq0, back, up, down, o, h, ext, sems, more,
):
    joint = open_qkv(0, info, wq_ref, (qa, qb, qd, qe), wq0, more)
    copies = open_rest(0, info, (wo, wu, wd), (a, b, d, e), back, up, down, sems)
    norm_all(0, first, gain_a, h)
    wait(joint)
    shuts = [shut_if(info[1] < 2)]
    for g in range(2):
        all_project(0, info, temps, h, wq0, None, kv0, g)
        at = g * 2 * HEAD
        spread_values(kv0, at, ext, 0)

        def one(rows, to, lanes, at=at):
            old = (acc_ref[rows, :], top_ref[rows, :1])
            acc, _ = soften(q_ref[rows, :], (kv0,), (at,), shuts, ext, old)
            o[to, lanes] = close(acc)

        each_head(g, one, False)
    wait(copies)
    finish_rows(0, x_ref, o, gain_m, back, up, down, out)


def first_kernel(
    info, temps, first, kv0, gain_a, gain_m, wq0, back, up, down, wq1,
    kv_out, q, o, x, h, ext,
):
    norm_all(0, first, gain_a, h)
    for g in range(2):
        all_project(0, info, temps, h, wq0, q, None, g)
        mix(q, (kv0,), (g * 2 * HEAD,), [None], o, ext, g)
    finish_rows(0, first, o, gain_m, back, up, down, x)
    norm_all(1, x, gain_a, h)
    for g in range(2):
        all_project(1, info, temps, h, wq1, None, kv_out, g)


def last_kernel(
    info, x_ref, q_ref, kv, prior, kv0, gain_m, wo, wu, wd, a, b, d, e,
    out, back, up, down, o, ext, sems,
):
    copies = open_rest(1, info, (wo, wu, wd), (a, b, d, e), back, up, down, sems)
    shuts = [None, shut_if(info[1] < 1), shut_if(info[1] < 2)]
    for g in range(2):
        mine, theirs = g * 2 * HEAD, (1 - g) * 2 * HEAD
        mix(q_ref, (kv, prior, kv0), (mine, theirs, mine), shuts, o, ext, g)
    wait(copies)
    finish_rows(1, x_ref, o, gain_m, back, up, down, out)


def ext_scratch(n):
    return pltpu.VMEM((n, S, 2 * HEAD), BF)


def shards(x, gain_a, wqkv, temps, wout, gain_m, wup, wdown):
    me = lax.axis_index(BOTH)
    info = jnp.stack([(me >> 1) & 1, me, me & 1]).astype(jnp.int32)
    x = x[0]
    own = (wout, wup, wdown)
    own_in = [(HBM, w) for w in own]
    sems = pltpu.SemaphoreType.DMA((15,))
    head = [(SMEM, info), (SMEM, temps)]

    def joint(l, x, quarters):
        return call(
            functools.partial(qkv_kernel, l),
            "qkv",
            [Q, KV, WQ] if l else [Q, KV],
            head + [(VMEM, x), (VMEM, gain_a), (HBM, wqkv)] + [(HBM, w) for w in quarters],
            4 * S * D * G,
            ([] if l else [pltpu.VMEM(WQ.shape, BF)]) + [pltpu.VMEM((S, D), BF), sems],
            16 if l else 48,
        )

    parts = []
    for l in range(2):
        parts += [[(0, l, NQ)], [(1, l, NO), (2, l, NU), (3, l, NU)]]
    p = cut(info, (wqkv, *own), parts)
    first, q, kv, prior, q0, r0, q1 = spread_first(x, p, joint)
    r0 = swap(r0)
    acc, top = call(
        begin_kernel,
        "begin",
        [jax.ShapeDtypeStruct((2 * RATIO * S, w), F32) for w in (2 * HEAD, HEAD)],
        [(SMEM, info), (VMEM, q), (VMEM, kv), (VMEM, prior)],
        8 * S * S * D,
        [ext_scratch(2)],
    )
    (acc, first), q1 = lax.optimization_barrier(((acc, first), q1))
    r1 = fetch(p[3], first)
    gains = [(VMEM, gain_a), (VMEM, gain_m)]
    x, kv0, wq, back, up, down = call(
        own_kernel,
        "own",
        [X, KV, WQ] + REST,
        head
        + [(VMEM, v) for v in (first, x, q, acc, top)]
        + gains
        + [(HBM, wqkv)]
        + [(HBM, w) for w in q0]
        + own_in
        + [(HBM, w) for w in r0],
        14 * S * D * D + 4 * S * S * D,
        [pltpu.VMEM((S, D), BF)] * 2 + [ext_scratch(1), sems, pltpu.SemaphoreType.DMA((5,))],
    )
    q, kv, wq1 = joint(1, x, swap(q1, acc))
    prior = send(kv, NEXT)
    weights = [(VMEM, w) for w in (wq, back, up, down)]
    r1 = swap(r1, kv)
    (kv0,) = call(
        first_kernel,
        "first",
        [KV],
        head
        + [(VMEM, first), (VMEM, kv0)]
        + gains
        + weights
        + [(VMEM, wq1)],
        14 * S * D * D + 4 * S * S * D,
        [pltpu.VMEM(Q.shape, BF)] + [pltpu.VMEM((S, D), BF)] * 3 + [ext_scratch(1)],
    )
    (x,) = call(
        last_kernel,
        "last",
        [X],
        [(SMEM, info)]
        + [(VMEM, v) for v in (x, q, kv, prior, kv0, gain_m)]
        + own_in
        + [(HBM, w) for w in r1],
        10 * S * D * D + 12 * S * S * D,
        [pltpu.VMEM(w.shape, BF) for w in REST] + [pltpu.VMEM((S, D), BF), ext_scratch(3), sems],
    )
    return x[None]


def solution(mesh):
    in_specs = (
        P(BOTH, None, None),
        P(),
        P(None, None, "mp"),
        P(),
        P(None, "mp", None),
        P(),
        P(None, None, "mp"),
        P(None, "mp", None),
    )
    return jax.shard_map(
        shards, mesh=mesh, in_specs=in_specs, out_specs=P(BOTH, None, None), check_vma=False
    )
```

```python
import functools
import math

import jax
import jax.numpy as jnp
from jax import lax
from jax.experimental import pallas as pl
from jax.experimental.pallas import tpu as pltpu
from jax.sharding import PartitionSpec as P


HEAD = 128
RATIO = 3
S = 384
D = 768
G = (RATIO + 2) * HEAD
BOTH = ("tm", "mp")
COUNT = 256
BF = jnp.bfloat16
F32 = jnp.float32
QSCALE = 1.0 / (math.sqrt(HEAD) * math.log(2.0))


def place(i):
    return (i >> 7) * 2 + (i & 1), (i >> 2) & 3, (i >> 4) & 7, (i >> 1) & 1


def index(x, y, z, c):
    return ((x >> 1) << 7) | (z << 4) | (y << 2) | (c << 1) | (x & 1)


def pairs(fn):
    return [(i, index(*fn(*place(i)))) for i in range(COUNT)]


X1 = pairs(lambda x, y, z, c: (x ^ 1, y, z, c))
X3 = pairs(lambda x, y, z, c: (x ^ 3, y, z, c))
Y1 = pairs(lambda x, y, z, c: (x, y ^ 1, z, c))
Y3 = pairs(lambda x, y, z, c: (x, y ^ 3, z, c))
Z1 = pairs(lambda x, y, z, c: (x, y, z ^ 1, c))
Z2 = pairs(lambda x, y, z, c: (x, y, z ^ 2, c))
Z6 = pairs(lambda x, y, z, c: (x, y, (((z + 2) & 7) ^ 2) - 2 & 7, c))
CORE = pairs(lambda x, y, z, c: (x, y, z, 1 - c))
NEXT = [(i, i + 1) for i in range(COUNT - 1)]


def send(v, p):
    return lax.ppermute(v, BOTH, p)


def spread_first(x, p, joint):
    me = lax.axis_index(BOTH)
    px, py, pz, pc = (me >> 7) * 2 + (me & 1), (me >> 2) & 3, (me >> 4) & 7, (me >> 1) & 1
    tie = lax.optimization_barrier
    half = D // 2
    got = send(x[:, half:], CORE)
    cur = jnp.where(pc == 0, x[:, :half], got)
    cur, p = tie((cur, p))
    q0 = fetch(p[0], None)
    cur = jnp.where(py == 0, cur[:192], send(cur[192:], Y3))
    cur = jnp.where((py == 0) | (py == 3), cur[:96], send(cur[96:], Y1))
    cur, q0 = tie((cur, q0))
    q0 = swap(q0)
    cur = jnp.where(pz == 0, cur[:48], send(cur[48:], Z1))
    cur = jnp.where(px == 0, cur, send(cur, X1))
    cur, q0 = tie((cur, q0))
    q, kv = joint(0, x, q0)
    cur = jnp.where(px < 2, cur, send(cur, X3))
    cur, kv = tie((cur, kv))
    prior = send(kv, NEXT)
    r0 = fetch(p[1], cur)
    a, b = send(cur, Z2), send(cur, Z6)
    cur = jnp.where(pz < 2, cur, jnp.where(pz < 4, a, b))
    got = send(cur, Z6)
    cur = jnp.where((pz == 4) | (pz == 5), got, cur)
    cur = jnp.concatenate([cur, send(cur, Z1)], axis=0)
    q1 = fetch(p[2], kv)
    cur = jnp.concatenate([cur, send(cur, Y1)], axis=0)
    cur = jnp.concatenate([cur, send(cur, Y3)], axis=0)
    got = send(cur, CORE)
    whole = jnp.where(
        pc == 0, jnp.concatenate([cur, got], axis=1), jnp.concatenate([got, cur], axis=1)
    )
    return whole, q, kv, prior, q0, r0, q1


VMEM = pl.BlockSpec(memory_space=pltpu.VMEM)
SMEM = pl.BlockSpec(memory_space=pltpu.SMEM)
ANY = pl.BlockSpec(memory_space=pl.ANY)
HBM = pl.BlockSpec(memory_space=pltpu.HBM)
NQ, NO, NU = 192, 96, 192


def params(mib=40):
    return pltpu.CompilerParams(vmem_limit_bytes=mib << 20)


def cost(flops, nbytes):
    return pl.CostEstimate(flops=flops, bytes_accessed=nbytes, transcendentals=0)


def cut_kernel(parts, info, *refs):
    k = 1 + max(i for part in parts for i, _, _ in part)
    n = len(parts)
    sources, outs, stages, sems = refs[:k], refs[k : k + 2 * n], refs[k + 2 * n : -1], refs[-1]
    core = info[0]
    at = 0
    loads = []
    for stage, part in zip(stages, parts):
        for j in range(2):
            to = 0
            group = []
            for i, l, rows in part:
                row = pl.multiple_of(core * (2 * rows) + j * rows, 16)
                group.append(
                    bring(
                        sources[i].at[l, pl.ds(row, rows)],
                        stage.at[j, pl.ds(to, rows)],
                        sems.at[at],
                    )
                )
                to += rows
                at += 1
            loads.append(group)
    stores = []
    for m, group in enumerate(loads):
        wait(group)
        stores.append(bring(stages[m // 2].at[m % 2], outs[m], sems.at[at]))
        at += 1
    wait(stores)


def cut(info, sources, parts):
    widths = [sources[part[0][0]].shape[2] for part in parts]
    heights = [sum(rows for _, _, rows in part) for part in parts]
    shapes = []
    for n, w in zip(heights, widths):
        shapes += [jax.ShapeDtypeStruct((n, w), BF)] * 2
    flat = pl.pallas_call(
        functools.partial(cut_kernel, parts),
        out_shape=shapes,
        in_specs=[SMEM] + [HBM] * len(sources),
        out_specs=[HBM] * len(shapes),
        scratch_shapes=[pltpu.VMEM((2, n, w), BF) for n, w in zip(heights, widths)]
        + [pltpu.SemaphoreType.DMA((2 * sum(len(part) + 1 for part in parts),))],
        compiler_params=params(63),
        name="cut",
    )(info, *sources)
    return [flat[2 * i : 2 * i + 2] for i in range(len(parts))]


def fetch(p, after=None):
    if after is not None:
        p, _ = lax.optimization_barrier((p, after))
    return send(p[0], X1), send(p[1], X3)


def swap(ab, after=None):
    if after is not None:
        ab, _ = lax.optimization_barrier((ab, after))
    return *ab, send(ab[0], CORE), send(ab[1], CORE)


def fill(info, quarters, at, n, dst, base, sems, first):
    width = dst.shape[1]
    copies = []
    for j, ref in enumerate(quarters):
        who = info[0] if j < 2 else 1 - info[0]
        row = pl.multiple_of(base + who * (2 * n) + (j % 2) * n, 16)
        c = pltpu.make_async_copy(
            ref.at[pl.ds(at, n), pl.ds(0, width)], dst.at[pl.ds(row, n)], sems.at[first + j]
        )
        c.start()
        copies.append(c)
    return copies


def bring(src, dst, sem):
    c = pltpu.make_async_copy(src, dst, sem)
    c.start()
    return c


def wait(copies):
    for c in copies:
        c.wait()


def rms(t, gain):
    scale = lax.rsqrt(jnp.mean(t * t, axis=-1, keepdims=True) + 1e-06)
    return (t * scale * gain).astype(BF)


def dot(a, b):
    return jnp.dot(a, b, preferred_element_type=F32)


def dot_t(a, b):
    return lax.dot_general(a, b, (((1,), (1,)), ((), ())), preferred_element_type=F32)


def head_norm(t):
    return t * lax.rsqrt(jnp.mean(t * t, axis=-1, keepdims=True) + 1e-06)


def open_qkv(l, info, wq, quarters, w, sems):
    return [bring(wq.at[l], w.at[pl.ds(0, D)], sems.at[4])] + fill(
        info, quarters, 0, NQ, w, D, sems, 0
    )


def open_rest(l, info, own, quarters, back, up, down, sems):
    wo, wu, wd = own
    copies = [bring(wo.at[l], back.at[pl.ds(0, S)], sems.at[12])]
    copies += fill(info, quarters, 0, NO, back, S, sems, 0)
    copies += [bring(wu.at[l], up.at[pl.ds(0, D)], sems.at[13])]
    copies += fill(info, quarters, NO, NU, up, D, sems, 4)
    copies += [bring(wd.at[l], down.at[pl.ds(0, D)], sems.at[14])]
    copies += fill(info, quarters, NO + NU, NU, down, D, sems, 8)
    return copies


def scales(info, temps, l, g):
    group = info[2] if g == 0 else 1 - info[2]
    return [temps[l, group * RATIO + r] * QSCALE for r in range(RATIO)]


def project(h, w, ts, q_ref, kv_ref, row, g, keys):
    n = h.shape[0]
    first = 0 if ts is not None else RATIO * HEAD
    last = G if keys else RATIO * HEAD
    raw = dot(h, w[pl.ds(g * D, D), first:last])
    if ts is not None:
        for r in range(RATIO):
            t = head_norm(raw[:, r * HEAD : (r + 1) * HEAD])
            q_ref[pl.ds((g * RATIO + r) * S + row, n), :] = (t * ts[r]).astype(BF)
    if keys:
        at = RATIO * HEAD - first
        kv_ref[pl.ds(row, n), pl.ds(g * 2 * HEAD, HEAD)] = head_norm(
            raw[:, at : at + HEAD]
        ).astype(BF)
        kv_ref[pl.ds(row, n), pl.ds(g * 2 * HEAD + HEAD, HEAD)] = raw[:, at + HEAD :].astype(BF)


QKV_STEP = 192
MIX_STEP = 384
END_STEP = 192
WQ = jax.ShapeDtypeStruct((2 * D, G), BF)
REST = [jax.ShapeDtypeStruct((n * D, D), BF) for n in (1, 2, 2)]
KV = jax.ShapeDtypeStruct((S, 4 * HEAD), BF)
Q = jax.ShapeDtypeStruct((2 * RATIO * S, HEAD), BF)
X = jax.ShapeDtypeStruct((S, D), BF)


def over(n, step, body, loop=False):
    if not loop:
        for row in range(0, n, step):
            body(row)
        return

    @pl.loop(0, n // step)
    def _(i):
        body(pl.multiple_of(i * step, step))


def norm_all(l, x_ref, gain, h):
    def one(row):
        rows = pl.ds(row, QKV_STEP)
        h[rows, :] = rms(x_ref[rows, :].astype(F32), gain[pl.ds(l, 1), :])

    over(S, QKV_STEP, one)


def all_project(l, info, temps, h, w, q_ref, kv_ref, g):
    ts = None if q_ref is None else scales(info, temps, l, g)

    def one(row):
        project(h[pl.ds(row, QKV_STEP), :], w, ts, q_ref, kv_ref, row, g, kv_ref is not None)

    over(S, QKV_STEP, one)


def call(body, outs, ins, flops, scratch=(), mib=16):
    return pl.pallas_call(
        body,
        out_shape=outs,
        in_specs=[spec for spec, _ in ins],
        out_specs=[VMEM] * len(outs),
        scratch_shapes=list(scratch),
        compiler_params=params(mib),
        cost_estimate=cost(flops, 8 << 20),
    )(*[v for _, v in ins])


def qkv_kernel(l, info, temps, x_ref, gain, wq, a, b, d, e, q_ref, kv_ref, w, h, sems):
    copies = open_qkv(l, info, wq, (a, b, d, e), w, sems)
    norm_all(l, x_ref, gain, h)
    copies[0].wait()
    all_project(l, info, temps, h, w, q_ref, kv_ref, 0)
    wait(copies[1:])
    all_project(l, info, temps, h, w, q_ref, kv_ref, 1)


def spread_values(kv, at, ext, i):
    ext[i, :, :HEAD] = kv[:, at + HEAD : at + 2 * HEAD]
    ext[i, :, HEAD:] = jnp.ones((S, HEAD), BF)


def each_head(g, body, loop):
    def one(h):
        for row in range(0, S, MIX_STEP):
            body(
                pl.ds(pl.multiple_of(h * S + row, MIX_STEP), MIX_STEP),
                pl.ds(row, MIX_STEP),
                pl.ds(pl.multiple_of(h * HEAD, HEAD), HEAD),
            )

    if loop:
        pl.loop(g * RATIO, (g + 1) * RATIO)(one)
    else:
        for h in range(g * RATIO, (g + 1) * RATIO):
            one(h)


def soften(q, kvs, columns, shuts, ext, old=None):
    scores = [dot_t(q, kv[:, at : at + HEAD]) for kv, at in zip(kvs, columns)]
    top = None if old is None else old[1]
    for s, shut in zip(scores, shuts):
        t = s.max(axis=-1, keepdims=True)
        t = t if shut is None else t - shut
        top = t if top is None else jnp.maximum(top, t)
    acc = None if old is None else old[0] * jnp.exp2(old[1] - top)
    for i, (s, shut) in enumerate(zip(scores, shuts)):
        base = top if shut is None else top + shut
        part = dot(jnp.exp2(s - base).astype(BF), ext[i])
        acc = part if acc is None else acc + part
    return acc, top


def close(acc):
    return (acc[:, :HEAD] / acc[:, HEAD:]).astype(BF)


def mix(q_ref, kvs, columns, shuts, o_ref, ext, g):
    for i, (kv, at) in enumerate(zip(kvs, columns)):
        spread_values(kv, at, ext, i)

    def one(rows, to, lanes):
        acc, _ = soften(q_ref[rows, :], kvs, columns, shuts, ext)
        o_ref[to, lanes] = close(acc)

    each_head(g, one, len(kvs) > 1)


def shut_if(bad):
    return jnp.where(bad, 1e30, 0.0)


def begin_kernel(info, q_ref, kv, prior, acc_ref, top_ref, ext):
    shuts = [None, shut_if(info[1] < 1)]
    for g in range(2):
        columns = (g * 2 * HEAD, (1 - g) * 2 * HEAD)
        for i, (v, at) in enumerate(zip((kv, prior), columns)):
            spread_values(v, at, ext, i)

        def one(rows, to, lanes, columns=columns):
            acc, top = soften(q_ref[rows, :], (kv, prior), columns, shuts, ext)
            acc_ref[rows, :] = acc
            top_ref[rows, :] = jnp.broadcast_to(top, (MIX_STEP, HEAD))

        each_head(g, one, True)


def finish_rows(l, x_ref, o_ref, gain, back, up, down, out):
    def one(row):
        rows = pl.ds(row, END_STEP)
        x = (x_ref[rows, :].astype(F32) + dot(o_ref[rows, :], back[...])).astype(BF)
        h = rms(x.astype(F32), gain[pl.ds(l, 1), :])
        y = x.astype(F32)
        for g in range(2):
            t = jax.nn.gelu(dot(h, up[pl.ds(g * D, D), :]), approximate=True).astype(BF)
            y = y + dot(t, down[pl.ds(g * D, D), :])
        out[rows, :] = y.astype(BF)

    over(S, END_STEP, one, True)


def own_kernel(
    info, temps, first, x_ref, q_ref, acc_ref, top_ref, gain_a, gain_m, wq_ref,
    qa, qb, qd, qe, wo, wu, wd, a, b, d, e, out, kv0, wq0, back, up, down, o, h, ext, sems, more,
):
    joint = open_qkv(0, info, wq_ref, (qa, qb, qd, qe), wq0, more)
    copies = open_rest(0, info, (wo, wu, wd), (a, b, d, e), back, up, down, sems)
    norm_all(0, first, gain_a, h)
    wait(joint)
    shuts = [shut_if(info[1] < 2)]
    for g in range(2):
        all_project(0, info, temps, h, wq0, None, kv0, g)
        at = g * 2 * HEAD
        spread_values(kv0, at, ext, 0)

        def one(rows, to, lanes, at=at):
            old = (acc_ref[rows, :], top_ref[rows, :1])
            acc, _ = soften(q_ref[rows, :], (kv0,), (at,), shuts, ext, old)
            o[to, lanes] = close(acc)

        each_head(g, one, False)
    wait(copies)
    finish_rows(0, x_ref, o, gain_m, back, up, down, out)


def first_kernel(
    info, temps, first, kv0, gain_a, gain_m, wq0, back, up, down, wq1,
    kv_out, q, o, x, h, ext,
):
    norm_all(0, first, gain_a, h)
    for g in range(2):
        all_project(0, info, temps, h, wq0, q, None, g)
        mix(q, (kv0,), (g * 2 * HEAD,), [None], o, ext, g)
    finish_rows(0, first, o, gain_m, back, up, down, x)
    norm_all(1, x, gain_a, h)
    for g in range(2):
        all_project(1, info, temps, h, wq1, None, kv_out, g)


def last_kernel(
    info, x_ref, q_ref, kv, prior, kv0, gain_m, wo, wu, wd, a, b, d, e,
    out, back, up, down, o, ext, sems,
):
    copies = open_rest(1, info, (wo, wu, wd), (a, b, d, e), back, up, down, sems)
    shuts = [None, shut_if(info[1] < 1), shut_if(info[1] < 2)]
    for g in range(2):
        mine, theirs = g * 2 * HEAD, (1 - g) * 2 * HEAD
        mix(q_ref, (kv, prior, kv0), (mine, theirs, mine), shuts, o, ext, g)
    wait(copies)
    finish_rows(1, x_ref, o, gain_m, back, up, down, out)


def ext_scratch(n):
    return pltpu.VMEM((n, S, 2 * HEAD), BF)


def program(x, gain_a, wqkv, temps, wout, gain_m, wup, wdown):
    me = lax.axis_index(BOTH)
    info = jnp.stack([(me >> 1) & 1, me, me & 1]).astype(jnp.int32)
    x = x[0]
    own = (wout, wup, wdown)
    own_in = [(HBM, w) for w in own]
    sems = pltpu.SemaphoreType.DMA((15,))
    head = [(SMEM, info), (SMEM, temps)]

    def joint(l, x, quarters):
        return call(
            functools.partial(qkv_kernel, l),
            [Q, KV, WQ] if l else [Q, KV],
            head + [(VMEM, x), (VMEM, gain_a), (HBM, wqkv)] + [(HBM, w) for w in quarters],
            4 * S * D * G,
            ([] if l else [pltpu.VMEM(WQ.shape, BF)]) + [pltpu.VMEM((S, D), BF), sems],
            16 if l else 48,
        )

    parts = []
    for l in range(2):
        parts += [[(0, l, NQ)], [(1, l, NO), (2, l, NU), (3, l, NU)]]
    p = cut(info, (wqkv, *own), parts)
    first, q, kv, prior, q0, r0, q1 = spread_first(x, p, joint)
    r0 = swap(r0)
    acc, top = call(
        begin_kernel,
        [jax.ShapeDtypeStruct((2 * RATIO * S, w), F32) for w in (2 * HEAD, HEAD)],
        [(SMEM, info), (VMEM, q), (VMEM, kv), (VMEM, prior)],
        8 * S * S * D,
        [ext_scratch(2)],
    )
    r1 = fetch(p[3], first)
    gains = [(VMEM, gain_a), (VMEM, gain_m)]
    x, kv0, wq, back, up, down = call(
        own_kernel,
        [X, KV, WQ] + REST,
        head
        + [(VMEM, v) for v in (first, x, q, acc, top)]
        + gains
        + [(HBM, wqkv)]
        + [(HBM, w) for w in q0]
        + own_in
        + [(HBM, w) for w in r0],
        14 * S * D * D + 4 * S * S * D,
        [pltpu.VMEM((S, D), BF)] * 2 + [ext_scratch(1), sems, pltpu.SemaphoreType.DMA((5,))],
    )
    q, kv, wq1 = joint(1, x, swap(q1, acc))
    prior = send(kv, NEXT)
    weights = [(VMEM, w) for w in (wq, back, up, down)]
    r1 = swap(r1, kv)
    (kv0,) = call(
        first_kernel,
        [KV],
        head
        + [(VMEM, first), (VMEM, kv0)]
        + gains
        + weights
        + [(VMEM, wq1)],
        14 * S * D * D + 4 * S * S * D,
        [pltpu.VMEM(Q.shape, BF)] + [pltpu.VMEM((S, D), BF)] * 3 + [ext_scratch(1)],
    )
    (x,) = call(
        last_kernel,
        [X],
        [(SMEM, info)]
        + [(VMEM, v) for v in (x, q, kv, prior, kv0, gain_m)]
        + own_in
        + [(HBM, w) for w in r1],
        10 * S * D * D + 12 * S * S * D,
        [pltpu.VMEM(w.shape, BF) for w in REST] + [pltpu.VMEM((S, D), BF), ext_scratch(3), sems],
    )
    return x[None]


def solution(mesh):
    in_specs = (
        P(BOTH, None, None),
        P(),
        P(None, None, "mp"),
        P(),
        P(None, "mp", None),
        P(),
        P(None, None, "mp"),
        P(None, "mp", None),
    )
    return jax.shard_map(
        program, mesh=mesh, in_specs=in_specs, out_specs=P(BOTH, None, None), check_vma=False
    )
```

```python
import functools
import math

import jax
import jax.numpy as jnp
from jax import lax
from jax.experimental import pallas as pl
from jax.experimental.pallas import tpu as pltpu
from jax.sharding import PartitionSpec as P


HEAD = 128
RATIO = 3
S = 384
D = 768
G = (RATIO + 2) * HEAD
BOTH = ("tm", "mp")
COUNT = 256
BF = jnp.bfloat16
F32 = jnp.float32
QSCALE = 1.0 / (math.sqrt(HEAD) * math.log(2.0))


def place(i):
    return (i >> 7) * 2 + (i & 1), (i >> 2) & 3, (i >> 4) & 7, (i >> 1) & 1


def index(x, y, z, c):
    return ((x >> 1) << 7) | (z << 4) | (y << 2) | (c << 1) | (x & 1)


def pairs(fn):
    return [(i, index(*fn(*place(i)))) for i in range(COUNT)]


X1 = pairs(lambda x, y, z, c: (x ^ 1, y, z, c))
X3 = pairs(lambda x, y, z, c: (x ^ 3, y, z, c))
Y1 = pairs(lambda x, y, z, c: (x, y ^ 1, z, c))
Y3 = pairs(lambda x, y, z, c: (x, y ^ 3, z, c))
Z1 = pairs(lambda x, y, z, c: (x, y, z ^ 1, c))
Z2 = pairs(lambda x, y, z, c: (x, y, z ^ 2, c))
Z6 = pairs(lambda x, y, z, c: (x, y, (((z + 2) & 7) ^ 2) - 2 & 7, c))
CORE = pairs(lambda x, y, z, c: (x, y, z, 1 - c))
NEXT = [(i, i + 1) for i in range(COUNT - 1)]


def send(v, p):
    return lax.ppermute(v, BOTH, p)


def spread_first(x, p, joint):
    me = lax.axis_index(BOTH)
    px, py, pz, pc = (me >> 7) * 2 + (me & 1), (me >> 2) & 3, (me >> 4) & 7, (me >> 1) & 1
    tie = lax.optimization_barrier
    half = D // 2
    got = send(x[:, half:], CORE)
    cur = jnp.where(pc == 0, x[:, :half], got)
    cur, p = tie((cur, p))
    q0 = fetch(p[0], None)
    cur = jnp.where(py == 0, cur[:192], send(cur[192:], Y3))
    cur = jnp.where((py == 0) | (py == 3), cur[:96], send(cur[96:], Y1))
    cur, q0 = tie((cur, q0))
    q0 = swap(q0)
    cur = jnp.where(pz == 0, cur[:48], send(cur[48:], Z1))
    cur = jnp.where(px == 0, cur, send(cur, X1))
    cur, q0 = tie((cur, q0))
    q, kv = joint(0, x, q0)
    cur = jnp.where(px < 2, cur, send(cur, X3))
    cur, kv = tie((cur, kv))
    prior = send(kv, NEXT)
    r0 = fetch(p[1], cur)
    a, b = send(cur, Z2), send(cur, Z6)
    cur = jnp.where(pz < 2, cur, jnp.where(pz < 4, a, b))
    got = send(cur, Z6)
    cur = jnp.where((pz == 4) | (pz == 5), got, cur)
    cur = jnp.concatenate([cur, send(cur, Z1)], axis=0)
    q1 = fetch(p[2], kv)
    late = kv
    cur = jnp.concatenate([cur, send(cur, Y1)], axis=0)
    cur = jnp.concatenate([cur, send(cur, Y3)], axis=0)
    got = send(cur, CORE)
    whole = jnp.where(
        pc == 0, jnp.concatenate([cur, got], axis=1), jnp.concatenate([got, cur], axis=1)
    )
    return whole, q, kv, prior, q0, r0, q1, late


VMEM = pl.BlockSpec(memory_space=pltpu.VMEM)
SMEM = pl.BlockSpec(memory_space=pltpu.SMEM)
ANY = pl.BlockSpec(memory_space=pl.ANY)
HBM = pl.BlockSpec(memory_space=pltpu.HBM)
NQ, NO, NU = 192, 96, 192


def params(mib=40):
    return pltpu.CompilerParams(vmem_limit_bytes=mib << 20)


def cost(flops, nbytes):
    return pl.CostEstimate(flops=flops, bytes_accessed=nbytes, transcendentals=0)


def cut_kernel(parts, info, *refs):
    k = 1 + max(i for part in parts for i, _, _ in part)
    n = len(parts)
    sources, outs, stages, sems = refs[:k], refs[k : k + 2 * n], refs[k + 2 * n : -1], refs[-1]
    core = info[0]
    at = 0
    loads = []
    for stage, part in zip(stages, parts):
        for j in range(2):
            to = 0
            group = []
            for i, l, rows in part:
                row = pl.multiple_of(core * (2 * rows) + j * rows, 16)
                group.append(
                    bring(
                        sources[i].at[l, pl.ds(row, rows)],
                        stage.at[j, pl.ds(to, rows)],
                        sems.at[at],
                    )
                )
                to += rows
                at += 1
            loads.append(group)
    stores = []
    for m, group in enumerate(loads):
        wait(group)
        stores.append(bring(stages[m // 2].at[m % 2], outs[m], sems.at[at]))
        at += 1
    wait(stores)


def cut(info, sources, parts):
    widths = [sources[part[0][0]].shape[2] for part in parts]
    heights = [sum(rows for _, _, rows in part) for part in parts]
    shapes = []
    for n, w in zip(heights, widths):
        shapes += [jax.ShapeDtypeStruct((n, w), BF)] * 2
    flat = pl.pallas_call(
        functools.partial(cut_kernel, parts),
        out_shape=shapes,
        in_specs=[SMEM] + [HBM] * len(sources),
        out_specs=[HBM] * len(shapes),
        scratch_shapes=[pltpu.VMEM((2, n, w), BF) for n, w in zip(heights, widths)]
        + [pltpu.SemaphoreType.DMA((2 * sum(len(part) + 1 for part in parts),))],
        compiler_params=params(63),
        name="cut",
    )(info, *sources)
    return [flat[2 * i : 2 * i + 2] for i in range(len(parts))]


def fetch(p, after=None):
    if after is not None:
        p, _ = lax.optimization_barrier((p, after))
    return send(p[0], X1), send(p[1], X3)


def swap(ab, after=None):
    if after is not None:
        ab, _ = lax.optimization_barrier((ab, after))
    return *ab, send(ab[0], CORE), send(ab[1], CORE)


def fill(info, quarters, at, n, dst, base, sems, first):
    width = dst.shape[1]
    copies = []
    for j, ref in enumerate(quarters):
        who = info[0] if j < 2 else 1 - info[0]
        row = pl.multiple_of(base + who * (2 * n) + (j % 2) * n, 16)
        c = pltpu.make_async_copy(
            ref.at[pl.ds(at, n), pl.ds(0, width)], dst.at[pl.ds(row, n)], sems.at[first + j]
        )
        c.start()
        copies.append(c)
    return copies


def bring(src, dst, sem):
    c = pltpu.make_async_copy(src, dst, sem)
    c.start()
    return c


def wait(copies):
    for c in copies:
        c.wait()


def rms(t, gain):
    scale = lax.rsqrt(jnp.mean(t * t, axis=-1, keepdims=True) + 1e-06)
    return (t * scale * gain).astype(BF)


def dot(a, b):
    return jnp.dot(a, b, preferred_element_type=F32)


def dot_t(a, b):
    return lax.dot_general(a, b, (((1,), (1,)), ((), ())), preferred_element_type=F32)


def head_norm(t):
    return t * lax.rsqrt(jnp.mean(t * t, axis=-1, keepdims=True) + 1e-06)


def open_qkv(l, info, wq, quarters, w, sems):
    return [bring(wq.at[l], w.at[pl.ds(0, D)], sems.at[4])] + fill(
        info, quarters, 0, NQ, w, D, sems, 0
    )


def open_rest(l, info, own, quarters, back, up, down, sems):
    wo, wu, wd = own
    copies = [bring(wo.at[l], back.at[pl.ds(0, S)], sems.at[12])]
    copies += fill(info, quarters, 0, NO, back, S, sems, 0)
    copies += [bring(wu.at[l], up.at[pl.ds(0, D)], sems.at[13])]
    copies += fill(info, quarters, NO, NU, up, D, sems, 4)
    copies += [bring(wd.at[l], down.at[pl.ds(0, D)], sems.at[14])]
    copies += fill(info, quarters, NO + NU, NU, down, D, sems, 8)
    return copies


def scales(info, temps, l, g):
    group = info[2] if g == 0 else 1 - info[2]
    return [temps[l, group * RATIO + r] * QSCALE for r in range(RATIO)]


def project(h, w, ts, q_ref, kv_ref, row, g, keys):
    n = h.shape[0]
    first = 0 if ts is not None else RATIO * HEAD
    last = G if keys else RATIO * HEAD
    raw = dot(h, w[pl.ds(g * D, D), first:last])
    if ts is not None:
        for r in range(RATIO):
            t = head_norm(raw[:, r * HEAD : (r + 1) * HEAD])
            q_ref[pl.ds((g * RATIO + r) * S + row, n), :] = (t * ts[r]).astype(BF)
    if keys:
        at = RATIO * HEAD - first
        kv_ref[pl.ds(row, n), pl.ds(g * 2 * HEAD, HEAD)] = head_norm(
            raw[:, at : at + HEAD]
        ).astype(BF)
        kv_ref[pl.ds(row, n), pl.ds(g * 2 * HEAD + HEAD, HEAD)] = raw[:, at + HEAD :].astype(BF)


QKV_STEP = 192
END_STEP = 192
WQ = jax.ShapeDtypeStruct((2 * D, G), BF)
REST = [jax.ShapeDtypeStruct((n * D, D), BF) for n in (1, 2, 2)]
KV = jax.ShapeDtypeStruct((S, 4 * HEAD), BF)
Q = jax.ShapeDtypeStruct((2 * RATIO * S, HEAD), BF)
X = jax.ShapeDtypeStruct((S, D), BF)


def over(n, step, body, loop=False):
    if not loop:
        for row in range(0, n, step):
            body(row)
        return

    @pl.loop(0, n // step)
    def _(i):
        body(pl.multiple_of(i * step, step))


def norm_all(l, x_ref, gain, h):
    def one(row):
        rows = pl.ds(row, QKV_STEP)
        h[rows, :] = rms(x_ref[rows, :].astype(F32), gain[pl.ds(l, 1), :])

    over(S, QKV_STEP, one)


def all_project(l, info, temps, h, w, q_ref, kv_ref, g):
    ts = None if q_ref is None else scales(info, temps, l, g)

    def one(row):
        project(h[pl.ds(row, QKV_STEP), :], w, ts, q_ref, kv_ref, row, g, kv_ref is not None)

    over(S, QKV_STEP, one)


def call(body, outs, ins, flops, scratch=(), mib=16):
    return pl.pallas_call(
        body,
        out_shape=outs,
        in_specs=[spec for spec, _ in ins],
        out_specs=[VMEM] * len(outs),
        scratch_shapes=list(scratch),
        compiler_params=params(mib),
        cost_estimate=cost(flops, 8 << 20),
    )(*[v for _, v in ins])


def qkv_kernel(l, info, temps, x_ref, gain, wq, a, b, d, e, q_ref, kv_ref, w, h, sems):
    copies = open_qkv(l, info, wq, (a, b, d, e), w, sems)
    norm_all(l, x_ref, gain, h)
    copies[0].wait()
    all_project(l, info, temps, h, w, q_ref, kv_ref, 0)
    wait(copies[1:])
    all_project(l, info, temps, h, w, q_ref, kv_ref, 1)


def spread_values(kv, at, ext, i):
    ext[i, :, :HEAD] = kv[:, at + HEAD : at + 2 * HEAD]
    ext[i, :, HEAD:] = jnp.ones((S, HEAD), BF)


def each_head(g, body, loop):
    step = S // 2 if loop else S

    def one(h):
        for row in range(0, S, step):
            body(
                pl.ds(pl.multiple_of(h * S + row, step), step),
                pl.ds(row, step),
                pl.ds(pl.multiple_of(h * HEAD, HEAD), HEAD),
            )

    if loop:
        pl.loop(g * RATIO, (g + 1) * RATIO)(one)
    else:
        for h in range(g * RATIO, (g + 1) * RATIO):
            one(h)


def soften(q, kvs, columns, shuts, ext, old=None):
    scores = [dot_t(q, kv[:, at : at + HEAD]) for kv, at in zip(kvs, columns)]
    top = None if old is None else old[1]
    for s, shut in zip(scores, shuts):
        t = s.max(axis=-1, keepdims=True)
        t = t if shut is None else t - shut
        top = t if top is None else jnp.maximum(top, t)
    acc = None if old is None else old[0] * jnp.exp2(old[1] - top)
    for i, (s, shut) in enumerate(zip(scores, shuts)):
        base = top if shut is None else top + shut
        part = dot(jnp.exp2(s - base).astype(BF), ext[i])
        acc = part if acc is None else acc + part
    return acc, top


def close(acc):
    return (acc[:, :HEAD] / acc[:, HEAD:]).astype(BF)


def mix(q_ref, kvs, columns, shuts, o_ref, ext, g):
    for i, (kv, at) in enumerate(zip(kvs, columns)):
        spread_values(kv, at, ext, i)

    def one(rows, to, lanes):
        acc, _ = soften(q_ref[rows, :], kvs, columns, shuts, ext)
        o_ref[to, lanes] = close(acc)

    each_head(g, one, len(kvs) > 1)


def shut_if(bad):
    return jnp.where(bad, 1e30, 0.0)


def begin_kernel(info, q_ref, kv, prior, acc_ref, top_ref, ext):
    shuts = [None, shut_if(info[1] < 1)]
    for g in range(2):
        columns = (g * 2 * HEAD, (1 - g) * 2 * HEAD)
        for i, (v, at) in enumerate(zip((kv, prior), columns)):
            spread_values(v, at, ext, i)

        def one(rows, to, lanes, columns=columns):
            acc, top = soften(q_ref[rows, :], (kv, prior), columns, shuts, ext)
            acc_ref[rows, :] = acc
            top_ref[rows, :] = jnp.broadcast_to(top, (top.shape[0], HEAD))

        each_head(g, one, True)


def finish_rows(l, x_ref, o_ref, gain, back, up, down, out):
    def one(row):
        rows = pl.ds(row, END_STEP)
        x = (x_ref[rows, :].astype(F32) + dot(o_ref[rows, :], back[...])).astype(BF)
        h = rms(x.astype(F32), gain[pl.ds(l, 1), :])
        y = x.astype(F32)
        for g in range(2):
            t = jax.nn.gelu(dot(h, up[pl.ds(g * D, D), :]), approximate=True).astype(BF)
            y = y + dot(t, down[pl.ds(g * D, D), :])
        out[rows, :] = y.astype(BF)

    over(S, END_STEP, one, True)


def own_kernel(
    info, temps, first, x_ref, q_ref, acc_ref, top_ref, gain_a, gain_m, wq_ref,
    qa, qb, qd, qe, wo, wu, wd, a, b, d, e, out, kv0, wq0, back, up, down, o, h, ext, sems, more,
):
    joint = open_qkv(0, info, wq_ref, (qa, qb, qd, qe), wq0, more)
    copies = open_rest(0, info, (wo, wu, wd), (a, b, d, e), back, up, down, sems)
    norm_all(0, first, gain_a, h)
    wait(joint)
    shuts = [shut_if(info[1] < 2)]
    for g in range(2):
        all_project(0, info, temps, h, wq0, None, kv0, g)
        at = g * 2 * HEAD
        spread_values(kv0, at, ext, 0)

        def one(rows, to, lanes, at=at):
            old = (acc_ref[rows, :], top_ref[rows, :1])
            acc, _ = soften(q_ref[rows, :], (kv0,), (at,), shuts, ext, old)
            o[to, lanes] = close(acc)

        each_head(g, one, False)
    wait(copies)
    finish_rows(0, x_ref, o, gain_m, back, up, down, out)


def first_kernel(
    info, temps, first, kv0, gain_a, gain_m, wq0, back, up, down, wq1,
    kv_out, q, o, x, h, ext,
):
    norm_all(0, first, gain_a, h)
    for g in range(2):
        all_project(0, info, temps, h, wq0, q, None, g)
        mix(q, (kv0,), (g * 2 * HEAD,), [None], o, ext, g)
    finish_rows(0, first, o, gain_m, back, up, down, x)
    norm_all(1, x, gain_a, h)
    for g in range(2):
        all_project(1, info, temps, h, wq1, None, kv_out, g)


def last_kernel(
    info, x_ref, q_ref, kv, prior, kv0, gain_m, wo, wu, wd, a, b, d, e,
    out, back, up, down, o, ext, sems,
):
    copies = open_rest(1, info, (wo, wu, wd), (a, b, d, e), back, up, down, sems)
    shuts = [None, shut_if(info[1] < 1), shut_if(info[1] < 2)]
    for g in range(2):
        mine, theirs = g * 2 * HEAD, (1 - g) * 2 * HEAD
        mix(q_ref, (kv, prior, kv0), (mine, theirs, mine), shuts, o, ext, g)
    wait(copies)
    finish_rows(1, x_ref, o, gain_m, back, up, down, out)


def ext_scratch(n):
    return pltpu.VMEM((n, S, 2 * HEAD), BF)


def program(x, gain_a, wqkv, temps, wout, gain_m, wup, wdown):
    me = lax.axis_index(BOTH)
    info = jnp.stack([(me >> 1) & 1, me, me & 1]).astype(jnp.int32)
    x = x[0]
    own = (wout, wup, wdown)
    own_in = [(HBM, w) for w in own]
    sems = pltpu.SemaphoreType.DMA((15,))
    head = [(SMEM, info), (SMEM, temps)]

    def joint(l, x, quarters):
        return call(
            functools.partial(qkv_kernel, l),
            [Q, KV, WQ] if l else [Q, KV],
            head + [(VMEM, x), (VMEM, gain_a), (HBM, wqkv)] + [(HBM, w) for w in quarters],
            4 * S * D * G,
            ([] if l else [pltpu.VMEM(WQ.shape, BF)]) + [pltpu.VMEM((S, D), BF), sems],
            16 if l else 48,
        )

    parts = []
    for l in range(2):
        parts += [[(0, l, NQ)], [(1, l, NO), (2, l, NU), (3, l, NU)]]
    p = cut(info, (wqkv, *own), parts)
    first, q, kv, prior, q0, r0, q1, late = spread_first(x, p, joint)
    r0 = swap(r0, None)
    acc, top = call(
        begin_kernel,
        [jax.ShapeDtypeStruct((2 * RATIO * S, w), F32) for w in (2 * HEAD, HEAD)],
        [(SMEM, info), (VMEM, q), (VMEM, kv), (VMEM, prior)],
        8 * S * S * D,
        [ext_scratch(2)],
    )
    r1 = fetch(p[3], late)
    gains = [(VMEM, gain_a), (VMEM, gain_m)]
    x, kv0, wq, back, up, down = call(
        own_kernel,
        [X, KV, WQ] + REST,
        head
        + [(VMEM, v) for v in (first, x, q, acc, top)]
        + gains
        + [(HBM, wqkv)]
        + [(HBM, w) for w in q0]
        + own_in
        + [(HBM, w) for w in r0],
        14 * S * D * D + 4 * S * S * D,
        [pltpu.VMEM((S, D), BF)] * 2 + [ext_scratch(1), sems, pltpu.SemaphoreType.DMA((5,))],
    )
    q, kv, wq1 = joint(1, x, swap(q1, acc))
    prior = send(kv, NEXT)
    weights = [(VMEM, w) for w in (wq, back, up, down)]
    r1 = swap(r1, kv)
    (kv0,) = call(
        first_kernel,
        [KV],
        head
        + [(VMEM, first), (VMEM, kv0)]
        + gains
        + weights
        + [(VMEM, wq1)],
        14 * S * D * D + 4 * S * S * D,
        [pltpu.VMEM(Q.shape, BF)] + [pltpu.VMEM((S, D), BF)] * 3 + [ext_scratch(1)],
    )
    (x,) = call(
        last_kernel,
        [X],
        [(SMEM, info)]
        + [(VMEM, v) for v in (x, q, kv, prior, kv0, gain_m)]
        + own_in
        + [(HBM, w) for w in r1],
        10 * S * D * D + 12 * S * S * D,
        [pltpu.VMEM(w.shape, BF) for w in REST] + [pltpu.VMEM((S, D), BF), ext_scratch(3), sems],
    )
    return x[None]


def solution(mesh):
    in_specs = (
        P(BOTH, None, None),
        P(),
        P(None, None, "mp"),
        P(),
        P(None, "mp", None),
        P(),
        P(None, None, "mp"),
        P(None, "mp", None),
    )
    return jax.shard_map(
        program, mesh=mesh, in_specs=in_specs, out_specs=P(BOTH, None, None), check_vma=False
    )
```
